32 devices in a mesh: ctx: 16 (over z, y, core), head: 2 (over x).
Axes of the slice: x: 2, y: 2, z: 4, core: 2. Of those that a mesh axis runs over, the one named last changes fastest.
Arguments:
- queries: bfloat16 [12288, 1024], P(('ctx', 'head')), may hold values from -64 to 64
- keys: bfloat16 [12288, 256], P(('ctx', 'head')), may hold values from -6 to 6
- values: bfloat16 [12288, 256], P(('ctx', 'head')), may hold values from -6 to 6
- out_grad: bfloat16 [12288, 1024], P(('ctx', 'head')), may hold values from -6 to 6
- rand_blocks: int32 [96, 3], replicated, may hold values from 0 to 95, as said below
- rand_count: int32 [96], replicated, may hold values from 1 to 3
Outputs:
- query_grad: bfloat16 [12288, 1024], P('ctx', 'head')
- key_grad: bfloat16 [12288, 256], P('ctx', 'head')
- value_grad: bfloat16 [12288, 256], P('ctx', 'head')
The draws below stay inside these ranges and needn't reach their ends.
Inputs may be any that keep to these rules, and one draw needn't show every extreme that they name: Entry rand_blocks[b, r] names a block of a ctx shard (a range of 6 blocks) that is neither b's own shard nor either neighbour of it, counted modulo 16. The 18 entries of one shard's query blocks name blocks of one other shard at most 2 times, exactly 2 times for some shard.
All inputs are finite; a program needn't handle non-finite values.
Results may differ from the reference program's by a relative error of at most 0.0087.
Values may be sent and summed in bfloat16 or wider, within the bound.
A program may use at most 64 MiB of HBM per device.

```python
import math
import jax
import jax.numpy as jnp
from jax import lax

BLOCK = 128
HD = 128
GROUP = 4
G = 2
RAND = 3
QB_DEV = 6
KV_HEADS = 2
HEADS = 8
NKB = 8
NQB = 96
TOKENS = 12288
N_CTX = 16


def shared_fields(key):
    folded = jax.random.fold_in(key, 101)
    field_key, query_key = jax.random.split(folded)
    key_width = KV_HEADS * HD
    key_field = jnp.clip(jax.random.normal(field_key, (TOKENS, key_width), jnp.float32), -6.0, 6.0)
    query_field = jnp.clip(jax.random.normal(query_key, (TOKENS, GROUP * key_width), jnp.float32), -6.0, 6.0)
    return (query_field, key_field)


def draw_queries(key, part):
    return shared_fields(key)[0].astype(jnp.bfloat16)


def draw_keys(key, part):
    return shared_fields(key)[1].astype(jnp.bfloat16)


def draw_rand_blocks(key, part):
    folded = jax.random.fold_in(key, 202)
    first_key, second_key, third_key = jax.random.split(folded, 3)
    entries = QB_DEV * RAND
    owners_used = min(entries, N_CTX - 3)
    candidates = jax.vmap(lambda single: jax.random.permutation(single, N_CTX - 3))(jax.random.split(first_key, N_CTX))
    shard_index = jnp.arange(N_CTX, dtype=jnp.int32)[:, None]
    candidates = (shard_index + 2 + candidates.astype(jnp.int32)) % N_CTX
    shuffle = jax.vmap(lambda single: jax.random.permutation(single, entries))(jax.random.split(second_key, N_CTX))
    slot_index = shuffle.astype(jnp.int32) % owners_used
    owners = jnp.take_along_axis(candidates, slot_index, axis=1)
    offset = jax.random.randint(third_key, (N_CTX, entries), 0, QB_DEV, dtype=jnp.int32)
    blocks = owners * QB_DEV + offset
    return blocks.reshape(NQB, RAND).astype(jnp.int32)


def plant(values, rng, low, largest):
    dims = values.shape
    spot = [jax.random.randint(jax.random.fold_in(rng, axis), (), 0, dims[axis]) for axis in range(len(dims))]
    values = values.at[tuple(spot)].set(low)
    longest = dims.index(max(dims))
    spot[longest] = (spot[longest] + 1) % dims[longest]
    return values.at[tuple(spot)].set(largest)


def shard_levels(rng, shape, cuts, low, top_value):
    factor_of = 1.0
    for dim, shards_of in cuts:
        steps = jax.random.uniform(jax.random.fold_in(jax.random.fold_in(rng, 6), dim), (shards_of,), jnp.float32, low / len(cuts), top_value / len(cuts))
        factor_of = factor_of * jnp.repeat(jnp.exp(steps), shape[dim] // shards_of).reshape((-1,) + (1,) * (len(shape) - 1 - dim))
    return factor_of


def centred(own_key, extent, scale, most, shards=(), held_as=jnp.bfloat16):
    drawn = scale * jax.random.normal(own_key, extent, jnp.float32)
    if shards:
        drawn = drawn * shard_levels(own_key, extent, shards, -0.22, 0.18)
    return jnp.clip(drawn, -most, most).astype(held_as)


def setup_inputs(seed: int = 0) -> dict:
    key_list = jax.random.split(jax.random.key(seed), 7)
    return {
        "queries": draw_queries(jax.random.fold_in(key_list[6], 71), 0),
        "keys": draw_keys(jax.random.fold_in(key_list[6], 71), 0),
        "values": centred(key_list[2], (TOKENS, KV_HEADS * HD), 1.0, 6.0, ((0, 32),)),
        "out_grad": centred(key_list[3], (TOKENS, HEADS * HD), 1.0, 6.0, ((0, 32),)),
        "rand_blocks": draw_rand_blocks(jax.random.fold_in(key_list[6], 71), 0),
        "rand_count": plant(jax.random.randint(key_list[5], (NQB,), 1, RAND + 1), jax.random.fold_in(key_list[5], 1), 1, RAND).astype(jnp.int32),
    }


def attend_block(query_tile, grad_tile, key_tile, value_tile, key_mask):
    factor = 1.0 / math.sqrt(HD)
    scores = jnp.einsum('tgh,kh->tgk', query_tile, key_tile) * factor
    scores = jnp.where(key_mask[None, None, :], scores, -jnp.inf)
    row_max = lax.optimization_barrier(jnp.max(scores, axis=-1, keepdims=True))
    raw_weights = jnp.exp(scores - row_max)
    weights = raw_weights / lax.optimization_barrier(jnp.sum(raw_weights, axis=-1, keepdims=True))
    weights_low = weights.astype(jnp.bfloat16).astype(jnp.float32)
    output = jnp.einsum('tgk,kh->tgh', weights_low, value_tile)
    row_dot = lax.optimization_barrier(jnp.sum(grad_tile * output, axis=-1, keepdims=True))
    dprobs = jnp.einsum('tgh,kh->tgk', grad_tile, value_tile)
    dscores = (weights * (dprobs - row_dot)).astype(jnp.bfloat16).astype(jnp.float32)
    dquery = (jnp.einsum('tgk,kh->tgh', dscores, key_tile) * factor).astype(jnp.bfloat16)
    key_part = jnp.einsum('tgk,tgh->kh', dscores, query_tile) * factor
    value_part = jnp.einsum('tgk,tgh->kh', weights_low, grad_tile)
    return (dquery, key_part, value_part)

def reference(queries, keys, values, out_grad, rand_blocks, rand_count):
    nblocks = rand_blocks.shape[0]
    query_all = queries.reshape(nblocks, BLOCK, KV_HEADS, GROUP, HD)
    grad_all = out_grad.reshape(nblocks, BLOCK, KV_HEADS, GROUP, HD)
    key_all = keys.reshape(nblocks, BLOCK, KV_HEADS, HD)
    value_all = values.reshape(nblocks, BLOCK, KV_HEADS, HD)
    dq_heads = []
    dk_heads = []
    dv_heads = []
    for head_id in range(KV_HEADS):
        query_head = query_all[:, :, head_id]
        grad_head = grad_all[:, :, head_id]
        key_head = key_all[:, :, head_id]
        value_head = value_all[:, :, head_id]

        def settle(part, remote):
            lowered = lax.optimization_barrier(part.astype(jnp.bfloat16)).astype(jnp.float32)
            return jnp.where(remote[:, None, None], lowered, part)

        def step(carry, block_id):
            key_acc, value_acc = carry
            window = jnp.stack([block_id - 1, block_id, block_id + 1]).astype(jnp.int32)
            key_table = jnp.concatenate([window, jnp.arange(G, dtype=jnp.int32), rand_blocks[block_id].astype(jnp.int32)])
            key_table = jnp.clip(key_table, 0, nblocks - 1)
            key_valid = jnp.concatenate([jnp.stack([block_id >= 1, block_id >= 0, block_id + 1 < nblocks]), jnp.ones((G,), bool), jnp.arange(RAND, dtype=jnp.int32) < rand_count[block_id]])
            remote = jnp.concatenate([jnp.stack([block_id % QB_DEV == 0, block_id < 0, block_id % QB_DEV == QB_DEV - 1]), jnp.zeros((G,), bool), jnp.ones((RAND,), bool)])
            key_tile = key_head[key_table].reshape(NKB * BLOCK, HD).astype(jnp.float32)
            value_tile = value_head[key_table].reshape(NKB * BLOCK, HD).astype(jnp.float32)
            key_mask = jnp.repeat(key_valid, BLOCK)
            query_tile = query_head[block_id].astype(jnp.float32)
            grad_tile = grad_head[block_id].astype(jnp.float32)
            dquery, key_part, value_part = attend_block(query_tile, grad_tile, key_tile, value_tile, key_mask)
            key_part = settle(key_part.reshape(NKB, BLOCK, HD), remote)
            value_part = settle(value_part.reshape(NKB, BLOCK, HD), remote)
            key_acc = key_acc.at[key_table].add(key_part)
            value_acc = value_acc.at[key_table].add(value_part)
            return ((key_acc, value_acc), dquery)
        zeros_acc = jnp.zeros((nblocks, BLOCK, HD), jnp.float32)
        (key_acc, value_acc), dq_blocks = lax.scan(step, (zeros_acc, zeros_acc), jnp.arange(nblocks, dtype=jnp.int32))
        dq_heads.append(dq_blocks)
        dk_heads.append(key_acc)
        dv_heads.append(value_acc)
    query_grad = jnp.stack(dq_heads, axis=2).reshape(nblocks * BLOCK, KV_HEADS * GROUP * HD)
    key_grad = jnp.stack(dk_heads, axis=2).reshape(nblocks * BLOCK, KV_HEADS * HD).astype(jnp.bfloat16)
    value_grad = jnp.stack(dv_heads, axis=2).reshape(nblocks * BLOCK, KV_HEADS * HD).astype(jnp.bfloat16)
    return (query_grad, key_grad, value_grad)
```

```python
import math

import jax
import jax.numpy as jnp
from jax import lax
from jax.experimental import pallas as pl
from jax.experimental.pallas import tpu as pltpu
from jax.sharding import PartitionSpec as P

BLOCK = 128
HD = 128
GROUP = 4
G = 2
RAND = 3
QB_DEV = 6
NKB = 8
FACTOR = 1.0 / math.sqrt(HD)
EXP_FACTOR = FACTOR * math.log2(math.e)
CONTRACT_LAST = (((1,), (1,)), ((), ()))
CONTRACT_FIRST = (((0,), (0,)), ((), ()))
CONTRACT_MATMUL = (((1,), (0,)), ((), ()))


def dot(a, b, dims=CONTRACT_MATMUL):
    return lax.dot_general(a, b, dims, preferred_element_type=jnp.float32)


def attend_kernel(
    table, valid, query_ref, grad_ref, pool_ref,
    dquery_ref, local_ref, far_ref, total, scores, dprobs, dscores, keys,
):
    step = pl.program_id(0)
    per_dev = local_ref.shape[0]

    @pl.when(step == 0)
    def _():
        total[...] = jnp.zeros_like(total)

    query = jnp.concatenate([query_ref[:, h * HD : (h + 1) * HD] for h in range(GROUP)], axis=0)
    grad = jnp.concatenate([grad_ref[:, h * HD : (h + 1) * HD] for h in range(GROUP)], axis=0)
    rows = [slice(e * BLOCK, (e + 1) * BLOCK) for e in range(NKB)]
    entry = [table[step, e] for e in range(NKB)]
    row_max = None
    for e in range(NKB):
        key_tile = pool_ref[entry[e], :, :HD]
        keys[rows[e], :] = key_tile
        bias = jnp.where(valid[step, e] > 0, 0.0, -jnp.inf).astype(jnp.float32)
        tile = dot(key_tile, query, CONTRACT_LAST) + bias
        scores[rows[e], :] = tile
        tile_max = jnp.max(tile, axis=0, keepdims=True)
        row_max = tile_max if e == 0 else jnp.maximum(row_max, tile_max)
    row_sum = jnp.zeros_like(row_max)
    row_dot = jnp.zeros_like(row_max)
    for e in range(NKB):
        weight = jnp.exp2((scores[rows[e], :] - row_max) * EXP_FACTOR)
        dprob = dot(pool_ref[entry[e], :, HD:], grad, CONTRACT_LAST)
        row_sum += jnp.sum(weight, axis=0, keepdims=True)
        row_dot += jnp.sum(weight * dprob, axis=0, keepdims=True)
        scores[rows[e], :] = weight
        dprobs[rows[e], :] = dprob
    scale = 1.0 / row_sum
    row_dot = row_dot * scale
    for e in range(NKB):
        weight = scores[rows[e], :] * scale
        dscore = (weight * (dprobs[rows[e], :] - row_dot)).astype(jnp.bfloat16)
        dscores[rows[e], :] = dscore
        total[entry[e], :, :HD] += dot(dscore, query) * FACTOR
        total[entry[e], :, HD:] += dot(weight.astype(jnp.bfloat16), grad)
    dquery = dot(keys[...], dscores[...], CONTRACT_FIRST) * FACTOR
    for h in range(GROUP):
        dquery_ref[:, h * HD : (h + 1) * HD] = dquery[:, h * BLOCK : (h + 1) * BLOCK].T.astype(
            jnp.bfloat16
        )

    @pl.when(step == pl.num_programs(0) - 1)
    def _():
        local_ref[...] = total[:per_dev]
        far_ref[...] = total[per_dev:].astype(jnp.bfloat16)


def attend(table, valid, queries, grads, pool):
    pool_size = pool.shape[0]
    per_dev = table.shape[0]
    tile = pl.BlockSpec((BLOCK, GROUP * HD), lambda i, *_: (i, 0))
    whole = lambda size: pl.BlockSpec((size, BLOCK, 2 * HD), lambda i, *_: (0, 0, 0), pipeline_mode=pl.Buffered(1))
    return pl.pallas_call(
        attend_kernel,
        grid_spec=pltpu.PrefetchScalarGridSpec(
            num_scalar_prefetch=2,
            grid=(per_dev,),
            in_specs=[tile, tile, whole(pool_size)],
            out_specs=[tile, whole(per_dev), whole(pool_size - per_dev)],
            scratch_shapes=[
                pltpu.VMEM((pool_size, BLOCK, 2 * HD), jnp.float32),
                pltpu.VMEM((NKB * BLOCK, GROUP * BLOCK), jnp.float32),
                pltpu.VMEM((NKB * BLOCK, GROUP * BLOCK), jnp.float32),
                pltpu.VMEM((NKB * BLOCK, GROUP * BLOCK), jnp.bfloat16),
                pltpu.VMEM((NKB * BLOCK, HD), jnp.bfloat16),
            ],
        ),
        out_shape=[
            jax.ShapeDtypeStruct(queries.shape, jnp.bfloat16),
            jax.ShapeDtypeStruct((per_dev, BLOCK, 2 * HD), jnp.float32),
            jax.ShapeDtypeStruct((pool_size - per_dev, BLOCK, 2 * HD), jnp.bfloat16),
        ],
        compiler_params=pltpu.CompilerParams(vmem_limit_bytes=48 << 20),
        name="attend",
    )(table, valid, queries, grads, pool)


def exchange(array):
    return lax.all_to_all(array, "ctx", split_axis=0, concat_axis=0, tiled=True)


def body(queries, keys, values, out_grad, rand_blocks, rand_count):
    heads = lax.axis_size("head")
    shards = lax.axis_size("ctx")
    myself = lax.axis_index("ctx")
    per_dev = QB_DEV
    entries = per_dev * RAND
    owners_used = min(entries, shards - 3)
    capacity = (entries + owners_used - 1) // owners_used
    total_blocks = per_dev * shards
    far_slots = shards * capacity
    piece = G * BLOCK // shards

    tokens = keys.shape[0]
    pairs = jnp.stack([keys.reshape(tokens, heads, HD), values.reshape(tokens, heads, HD)], axis=2)
    pairs = pairs.transpose(1, 0, 2, 3).reshape(heads, tokens, 2 * HD)
    local_rows = lax.all_to_all(pairs, "head", split_axis=0, concat_axis=0, tiled=True)
    local_rows = local_rows.reshape(heads * tokens, 2 * HD)
    local_pairs = local_rows.reshape(per_dev, BLOCK, 2 * HD)
    head_queries = lax.all_to_all(queries, "head", split_axis=1, concat_axis=0, tiled=True)
    head_grads = lax.all_to_all(out_grad, "head", split_axis=1, concat_axis=0, tiled=True)

    flat_blocks = rand_blocks.reshape(shards, entries)
    owners = flat_blocks // per_dev
    offsets = flat_blocks % per_dev
    positions = jnp.arange(entries, dtype=jnp.int32)
    earlier = positions[None, :] < positions[:, None]
    same_owner = owners[:, :, None] == owners[:, None, :]
    slot_ranks = jnp.sum(same_owner & earlier[None], axis=2)
    slot_range = jnp.arange(capacity, dtype=jnp.int32)
    send_hits = (
        (owners == myself)[:, None, :] & (slot_ranks[:, None, :] == slot_range[None, :, None])
    ).astype(jnp.float32)
    offset_hot = (
        offsets[:, :, None] == jnp.arange(per_dev, dtype=jnp.int32)[None, None, :]
    ).astype(jnp.float32)
    send_table = jnp.einsum("dme,deq->dmq", send_hits, offset_hot)
    targets = jnp.arange(shards, dtype=jnp.int32)[:, None, None]
    first_slot = (slot_range == 0)[None, :, None]
    block_range = jnp.arange(per_dev, dtype=jnp.int32)[None, None, :]
    right_send = (targets == (myself + 1) % shards) & first_slot & (block_range == per_dev - 1)
    left_send = (targets == (myself - 1 + shards) % shards) & first_slot & (block_range == 0)
    send_table = send_table + right_send.astype(jnp.float32) + left_send.astype(jnp.float32)
    left_far = per_dev + (myself - 1 + shards) % shards * capacity
    right_far = per_dev + (myself + 1) % shards * capacity
    outgoing = jnp.einsum(
        "dmq,qtc->dmtc",
        send_table.astype(jnp.bfloat16),
        local_pairs,
        preferred_element_type=jnp.float32,
    ).astype(jnp.bfloat16)
    pieces = local_rows[: G * BLOCK].reshape(shards, piece, 2 * HD)
    packed = jnp.concatenate([outgoing.reshape(shards, capacity * BLOCK, 2 * HD), pieces], axis=1)
    arrived = exchange(packed)
    far_pairs = arrived[:, : capacity * BLOCK].reshape(far_slots, BLOCK, 2 * HD)
    my_piece = jnp.broadcast_to(arrived[0, capacity * BLOCK :][None], (shards, piece, 2 * HD))
    global_pairs = exchange(my_piece).reshape(G, BLOCK, 2 * HD)
    pool = jnp.concatenate([local_pairs, far_pairs, global_pairs], axis=0)

    edge_base = per_dev + far_slots
    local_index = jnp.arange(per_dev, dtype=jnp.int32)
    seq_block = myself * per_dev + local_index
    left_index = jnp.where(local_index > 0, local_index - 1, left_far)
    right_index = jnp.where(local_index < per_dev - 1, local_index + 1, right_far)
    global_index = jnp.broadcast_to(
        edge_base + jnp.arange(G, dtype=jnp.int32)[None, :], (per_dev, G)
    )
    my_owners = lax.dynamic_index_in_dim(owners, myself, 0, keepdims=False)
    my_ranks = lax.dynamic_index_in_dim(slot_ranks, myself, 0, keepdims=False)
    random_index = (per_dev + my_owners * capacity + my_ranks).reshape(per_dev, RAND)
    key_table = jnp.concatenate(
        [jnp.stack([left_index, local_index, right_index], axis=1), global_index, random_index],
        axis=1,
    ).astype(jnp.int32)
    my_counts = lax.dynamic_slice_in_dim(rand_count, myself * per_dev, per_dev)
    key_valid = jnp.concatenate(
        [
            jnp.stack([seq_block > 0, seq_block >= 0, seq_block < total_blocks - 1], axis=1),
            jnp.ones((per_dev, G), bool),
            jnp.arange(RAND, dtype=jnp.int32)[None, :] < my_counts[:, None],
        ],
        axis=1,
    ).astype(jnp.int32)

    query_grad, local_grads, far_grads = attend(key_table, key_valid, head_queries, head_grads, pool)

    packed_grads = jnp.concatenate(
        [
            far_grads[:far_slots].reshape(shards, capacity * BLOCK, 2 * HD),
            far_grads[far_slots:].reshape(shards, piece, 2 * HD),
        ],
        axis=1,
    )
    returned = exchange(packed_grads)
    returned_far = returned[:, : capacity * BLOCK].reshape(shards, capacity, BLOCK, 2 * HD)
    global_piece = jnp.sum(returned[:, capacity * BLOCK :].astype(jnp.float32), axis=0)
    global_piece = jnp.broadcast_to(global_piece[None].astype(jnp.bfloat16), (shards, piece, 2 * HD))
    global_total = exchange(global_piece).reshape(G, BLOCK, 2 * HD).astype(jnp.float32)
    local_grads = local_grads + jnp.einsum(
        "dmq,dmtc->qtc",
        send_table.astype(jnp.bfloat16),
        returned_far,
        preferred_element_type=jnp.float32,
    )
    local_grads = local_grads.at[:G].add(
        jnp.where(myself == 0, global_total, jnp.zeros_like(global_total))
    )
    key_grad = local_grads[:, :, :HD].reshape(per_dev * BLOCK, HD).astype(jnp.bfloat16)
    value_grad = local_grads[:, :, HD:].reshape(per_dev * BLOCK, HD).astype(jnp.bfloat16)
    return (query_grad, key_grad, value_grad)


def solution(mesh):
    placed = P(("ctx", "head"), None)
    return jax.shard_map(
        body,
        mesh=mesh,
        in_specs=(placed, placed, placed, placed, P(), P()),
        out_specs=(P("ctx", "head"), P("ctx", "head"), P("ctx", "head")),
        check_vma=False,
    )
```

```python
import functools
import math

import jax
import jax.numpy as jnp
from jax import lax
from jax.experimental import pallas as pl
from jax.experimental.pallas import tpu as pltpu
from jax.sharding import PartitionSpec as P

BLOCK = 128
HD = 128
GROUP = 4
G = 2
RAND = 3
QB_DEV = 6
NKB = 8
FACTOR = 1.0 / math.sqrt(HD)
EXP_FACTOR = FACTOR * math.log2(math.e)
CONTRACT_LAST = (((1,), (1,)), ((), ()))
CONTRACT_FIRST = (((0,), (0,)), ((), ()))
CONTRACT_MATMUL = (((1,), (0,)), ((), ()))


def dot(a, b, dims=CONTRACT_MATMUL):
    return lax.dot_general(a, b, dims, preferred_element_type=jnp.float32)


def attend_kernel(
    direct, table, valid, query_ref, grad_ref, pool_ref,
    dquery_ref, local_ref, far_ref, total, scores, dprobs, dscores, keys,
):
    step = pl.program_id(0)
    per_dev = local_ref.shape[0]
    first = 0
    if direct:
        first = lax.axis_index("ctx") * per_dev
        block = first + step
        last = pool_ref.shape[0] - 1
        entry = [jnp.maximum(block - 1, 0), block, jnp.minimum(block + 1, last), 0, 1]
        entry += [table[block, r] for r in range(RAND)]
        use = [block > 0, True, block < last, True, True]
        use += [r < valid[block] for r in range(RAND)]
    else:
        entry = [table[step, e] for e in range(NKB)]
        use = [valid[step, e] > 0 for e in range(NKB)]

    @pl.when(step == 0)
    def _():
        total[...] = jnp.zeros_like(total)

    query = jnp.concatenate([query_ref[:, h * HD : (h + 1) * HD] for h in range(GROUP)], axis=0)
    grad = jnp.concatenate([grad_ref[:, h * HD : (h + 1) * HD] for h in range(GROUP)], axis=0)
    rows = [slice(e * BLOCK, (e + 1) * BLOCK) for e in range(NKB)]
    row_max = None
    for e in range(NKB):
        key_tile = pool_ref[entry[e], :, :HD]
        keys[rows[e], :] = key_tile
        tile = dot(key_tile, query, CONTRACT_LAST)
        if use[e] is not True:
            tile += jnp.where(use[e], 0.0, -jnp.inf).astype(jnp.float32)
        scores[rows[e], :] = tile
        tile_max = jnp.max(tile, axis=0, keepdims=True)
        row_max = tile_max if e == 0 else jnp.maximum(row_max, tile_max)
    row_sum = jnp.zeros_like(row_max)
    row_dot = jnp.zeros_like(row_max)
    for e in range(NKB):
        weight = jnp.exp2((scores[rows[e], :] - row_max) * EXP_FACTOR)
        dprob = dot(pool_ref[entry[e], :, HD:], grad, CONTRACT_LAST)
        row_sum += jnp.sum(weight, axis=0, keepdims=True)
        row_dot += jnp.sum(weight * dprob, axis=0, keepdims=True)
        scores[rows[e], :] = weight
        dprobs[rows[e], :] = dprob
    scale = 1.0 / row_sum
    row_dot = row_dot * scale
    for e in range(NKB):
        weight = scores[rows[e], :] * scale
        dscore = (weight * (dprobs[rows[e], :] - row_dot)).astype(jnp.bfloat16)
        dscores[rows[e], :] = dscore
        total[entry[e], :, :HD] += dot(dscore, query) * FACTOR
        total[entry[e], :, HD:] += dot(weight.astype(jnp.bfloat16), grad)
    dquery = dot(keys[...], dscores[...], CONTRACT_FIRST) * FACTOR
    for h in range(GROUP):
        dquery_ref[:, h * HD : (h + 1) * HD] = dquery[:, h * BLOCK : (h + 1) * BLOCK].T.astype(
            jnp.bfloat16
        )

    @pl.when(step == pl.num_programs(0) - 1)
    def _():
        local_ref[...] = total[pl.ds(first, per_dev)]
        skip = total.shape[0] - far_ref.shape[0]

        @pl.loop(0, far_ref.shape[0])
        def _(i):
            far_ref[i] = total[skip + i].astype(jnp.bfloat16)


def attend(table, valid, queries, grads, pool, direct=False):
    pool_size = pool.shape[0]
    per_dev = QB_DEV
    far_size = pool_size if direct else pool_size - per_dev
    tile = pl.BlockSpec((BLOCK, GROUP * HD), lambda i, *_: (i, 0))
    whole = lambda size: pl.BlockSpec((size, BLOCK, 2 * HD), lambda i, *_: (0, 0, 0), pipeline_mode=pl.Buffered(1))
    return pl.pallas_call(
        functools.partial(attend_kernel, direct),
        grid_spec=pltpu.PrefetchScalarGridSpec(
            num_scalar_prefetch=2,
            grid=(per_dev,),
            in_specs=[tile, tile, whole(pool_size)],
            out_specs=[tile, whole(per_dev), whole(far_size)],
            scratch_shapes=[
                pltpu.VMEM((pool_size, BLOCK, 2 * HD), jnp.float32),
                pltpu.VMEM((NKB * BLOCK, GROUP * BLOCK), jnp.float32),
                pltpu.VMEM((NKB * BLOCK, GROUP * BLOCK), jnp.float32),
                pltpu.VMEM((NKB * BLOCK, GROUP * BLOCK), jnp.bfloat16),
                pltpu.VMEM((NKB * BLOCK, HD), jnp.bfloat16),
            ],
        ),
        out_shape=[
            jax.ShapeDtypeStruct(queries.shape, jnp.bfloat16),
            jax.ShapeDtypeStruct((per_dev, BLOCK, 2 * HD), jnp.float32),
            jax.ShapeDtypeStruct((far_size, BLOCK, 2 * HD), jnp.bfloat16),
        ],
        compiler_params=pltpu.CompilerParams(vmem_limit_bytes=48 << 20),
        name="attend",
    )(table, valid, queries, grads, pool)


def exchange(array):
    return lax.all_to_all(array, "ctx", split_axis=0, concat_axis=0, tiled=True)


def body(queries, keys, values, out_grad, rand_blocks, rand_count):
    heads = lax.axis_size("head")
    shards = lax.axis_size("ctx")
    myself = lax.axis_index("ctx")
    per_dev = QB_DEV
    entries = per_dev * RAND
    owners_used = min(entries, shards - 3)
    capacity = (entries + owners_used - 1) // owners_used
    total_blocks = per_dev * shards
    far_slots = shards * capacity
    piece = G * BLOCK // shards

    tokens = keys.shape[0]
    pairs = jnp.stack([keys.reshape(tokens, heads, HD), values.reshape(tokens, heads, HD)], axis=2)
    pairs = pairs.transpose(1, 0, 2, 3).reshape(heads, tokens, 2 * HD)
    local_rows = lax.all_to_all(pairs, "head", split_axis=0, concat_axis=0, tiled=True)
    local_rows = local_rows.reshape(heads * tokens, 2 * HD)
    local_pairs = local_rows.reshape(per_dev, BLOCK, 2 * HD)
    head_queries = lax.all_to_all(queries, "head", split_axis=1, concat_axis=0, tiled=True)
    head_grads = lax.all_to_all(out_grad, "head", split_axis=1, concat_axis=0, tiled=True)

    flat_blocks = rand_blocks.reshape(shards, entries)
    owners = flat_blocks // per_dev
    offsets = flat_blocks % per_dev
    positions = jnp.arange(entries, dtype=jnp.int32)
    earlier = positions[None, :] < positions[:, None]
    same_owner = owners[:, :, None] == owners[:, None, :]
    slot_ranks = jnp.sum(same_owner & earlier[None], axis=2)
    slot_range = jnp.arange(capacity, dtype=jnp.int32)
    send_hits = (
        (owners == myself)[:, None, :] & (slot_ranks[:, None, :] == slot_range[None, :, None])
    ).astype(jnp.float32)
    offset_hot = (
        offsets[:, :, None] == jnp.arange(per_dev, dtype=jnp.int32)[None, None, :]
    ).astype(jnp.float32)
    send_table = jnp.einsum("dme,deq->dmq", send_hits, offset_hot)
    targets = jnp.arange(shards, dtype=jnp.int32)[:, None, None]
    first_slot = (slot_range == 0)[None, :, None]
    block_range = jnp.arange(per_dev, dtype=jnp.int32)[None, None, :]
    right_send = (targets == (myself + 1) % shards) & first_slot & (block_range == per_dev - 1)
    left_send = (targets == (myself - 1 + shards) % shards) & first_slot & (block_range == 0)
    send_table = send_table + right_send.astype(jnp.float32) + left_send.astype(jnp.float32)
    left_far = per_dev + (myself - 1 + shards) % shards * capacity
    right_far = per_dev + (myself + 1) % shards * capacity
    outgoing = jnp.einsum(
        "dmq,qtc->dmtc",
        send_table.astype(jnp.bfloat16),
        local_pairs,
        preferred_element_type=jnp.float32,
    ).astype(jnp.bfloat16)
    pieces = local_rows[: G * BLOCK].reshape(shards, piece, 2 * HD)
    packed = jnp.concatenate([outgoing.reshape(shards, capacity * BLOCK, 2 * HD), pieces], axis=1)
    arrived = exchange(packed)
    far_pairs = arrived[:, : capacity * BLOCK].reshape(far_slots, BLOCK, 2 * HD)
    my_piece = jnp.broadcast_to(arrived[0, capacity * BLOCK :][None], (shards, piece, 2 * HD))
    global_pairs = exchange(my_piece).reshape(G, BLOCK, 2 * HD)
    pool = jnp.concatenate([local_pairs, far_pairs, global_pairs], axis=0)

    edge_base = per_dev + far_slots
    local_index = jnp.arange(per_dev, dtype=jnp.int32)
    seq_block = myself * per_dev + local_index
    left_index = jnp.where(local_index > 0, local_index - 1, left_far)
    right_index = jnp.where(local_index < per_dev - 1, local_index + 1, right_far)
    global_index = jnp.broadcast_to(
        edge_base + jnp.arange(G, dtype=jnp.int32)[None, :], (per_dev, G)
    )
    my_owners = lax.dynamic_index_in_dim(owners, myself, 0, keepdims=False)
    my_ranks = lax.dynamic_index_in_dim(slot_ranks, myself, 0, keepdims=False)
    random_index = (per_dev + my_owners * capacity + my_ranks).reshape(per_dev, RAND)
    key_table = jnp.concatenate(
        [jnp.stack([left_index, local_index, right_index], axis=1), global_index, random_index],
        axis=1,
    ).astype(jnp.int32)
    my_counts = lax.dynamic_slice_in_dim(rand_count, myself * per_dev, per_dev)
    key_valid = jnp.concatenate(
        [
            jnp.stack([seq_block > 0, seq_block >= 0, seq_block < total_blocks - 1], axis=1),
            jnp.ones((per_dev, G), bool),
            jnp.arange(RAND, dtype=jnp.int32)[None, :] < my_counts[:, None],
        ],
        axis=1,
    ).astype(jnp.int32)

    query_grad, local_grads, far_grads = attend(key_table, key_valid, head_queries, head_grads, pool)

    packed_grads = jnp.concatenate(
        [
            far_grads[:far_slots].reshape(shards, capacity * BLOCK, 2 * HD),
            far_grads[far_slots:].reshape(shards, piece, 2 * HD),
        ],
        axis=1,
    )
    returned = exchange(packed_grads)
    returned_far = returned[:, : capacity * BLOCK].reshape(shards, capacity, BLOCK, 2 * HD)
    global_piece = jnp.sum(returned[:, capacity * BLOCK :].astype(jnp.float32), axis=0)
    global_piece = jnp.broadcast_to(global_piece[None].astype(jnp.bfloat16), (shards, piece, 2 * HD))
    global_total = exchange(global_piece).reshape(G, BLOCK, 2 * HD).astype(jnp.float32)
    local_grads = local_grads + jnp.einsum(
        "dmq,dmtc->qtc",
        send_table.astype(jnp.bfloat16),
        returned_far,
        preferred_element_type=jnp.float32,
    )
    local_grads = local_grads.at[:G].add(
        jnp.where(myself == 0, global_total, jnp.zeros_like(global_total))
    )
    key_grad = local_grads[:, :, :HD].reshape(per_dev * BLOCK, HD).astype(jnp.bfloat16)
    value_grad = local_grads[:, :, HD:].reshape(per_dev * BLOCK, HD).astype(jnp.bfloat16)
    return (query_grad, key_grad, value_grad)

MESH = pl.DeviceIdType.MESH
LINE = 4
SHARD = QB_DEV * BLOCK


def place():
    me = lax.axis_index("ctx")
    return me // 4, (me // 2) % 2, me % 2


def index_of(z, y, c):
    return z * 4 + y * 2 + c


def remote(src, dst, send_sem, recv_sem, **device):
    return pltpu.make_async_remote_copy(
        src_ref=src, dst_ref=dst, send_sem=send_sem, recv_sem=recv_sem, device_id=device, device_id_type=MESH
    )


def greet(z, y, c, head):
    barrier = pltpu.get_barrier_semaphore()

    def tell(**device):
        pl.semaphore_signal(barrier, inc=1, device_id=device, device_id_type=MESH)

    tell(ctx=index_of(z, 1 - y, c))
    tell(ctx=index_of(z, y, 1 - c))
    if head is not None:
        tell(head=1 - head)

    @pl.when(z > 0)
    def _():
        tell(ctx=index_of(z - 1, y, c))

    @pl.when(z < LINE - 1)
    def _():
        tell(ctx=index_of(z + 1, y, c))

    peers = (2 if head is None else 3) + (z + 2) // 3 + (5 - z) // 3
    pl.semaphore_wait(barrier, peers)


def gather_kernel(
    q_in, k_in, v_in, g_in, q_out, g_out, pool,
    local_sem, head_send, head_recv, up_send, down_send, y_send, c_send, z_recv, y_recv, c_recv,
):
    z, y, c = place()
    me = index_of(z, y, c)
    head = lax.axis_index("head")
    other = 1 - head
    tokens = k_in.shape[0]

    def chunk(zz, yy, cc):
        return pool.at[pl.ds(pl.multiple_of(index_of(zz, yy, cc) * SHARD, SHARD), SHARD), :]

    pool_rows = pl.ds(pl.multiple_of(me * SHARD + head * tokens, tokens), tokens)
    out_rows = pl.ds(pl.multiple_of(head * tokens, tokens), tokens)
    jobs = []
    for src, dst, width in (
        (k_in, pool.at[pool_rows, :HD], HD),
        (v_in, pool.at[pool_rows, HD:], HD),
        (q_in, q_out.at[out_rows, :], GROUP * HD),
        (g_in, g_out.at[out_rows, :], GROUP * HD),
    ):
        i = len(jobs)
        mine = src.at[:, pl.ds(pl.multiple_of(head * width, width), width)]
        theirs = src.at[:, pl.ds(pl.multiple_of(other * width, width), width)]
        jobs.append(
            (
                pltpu.make_async_copy(mine, dst, local_sem.at[i]),
                remote(theirs, dst, head_send.at[i], head_recv.at[i], head=other),
            )
        )
    for local, _ in jobs:
        local.start()
    greet(z, y, c, head)
    for _, away in jobs:
        away.start()

    def up(zz):
        part = chunk(zz, y, c)
        return remote(part, part, up_send.at[zz], z_recv.at[zz], ctx=index_of((z + 1) % LINE, y, c))

    def down(zz):
        part = chunk(zz, y, c)
        return remote(part, part, down_send.at[zz], z_recv.at[zz], ctx=index_of((z + 3) % LINE, y, c))

    def across(zz):
        part = chunk(zz, y, c)
        return remote(part, part, y_send.at[zz], y_recv.at[zz], ctx=index_of(z, 1 - y, c))

    def beside(zz, yy):
        part = chunk(zz, yy, c)
        slot = zz * 2 + yy
        return remote(part, part, c_send.at[slot], c_recv.at[slot], ctx=index_of(z, y, 1 - c))

    for local, away in jobs[:2]:
        local.wait()
        away.wait_recv()

    @pl.when(z < LINE - 1)
    def _():
        up(z).start()

    @pl.when(z > 0)
    def _():
        down(z).start()

    across(z).start()
    beside(z, y).start()

    def from_partner(zz):
        across(zz).wait_recv()
        beside(zz, 1 - y).start()

    def stage(j, below, above):
        @pl.when(z - j >= 0)
        def _():
            below(z - j)

        @pl.when(z + j <= LINE - 1)
        def _():
            above(z + j)

    def from_below(zz):
        up(zz).wait_recv()

        @pl.when(z < LINE - 1)
        def _():
            up(zz).start()

        across(zz).start()
        beside(zz, y).start()

    def from_above(zz):
        down(zz).wait_recv()

        @pl.when(z > 0)
        def _():
            down(zz).start()

        across(zz).start()
        beside(zz, y).start()

    for j in range(1, LINE):
        stage(j, from_below, from_above)
        if j == 1:
            from_partner(z)
        else:
            stage(j - 1, from_partner, from_partner)
    stage(LINE - 1, from_partner, from_partner)

    for zz in range(LINE):
        for yy in range(2):
            beside(zz, yy).wait_recv()
            beside(zz, yy).wait_send()
        across(zz).wait_send()

        @pl.when((z < LINE - 1) & (zz <= z))
        def _():
            up(zz).wait_send()

        @pl.when((z > 0) & (zz >= z))
        def _():
            down(zz).wait_send()

    for i, (local, away) in enumerate(jobs):
        if i >= 2:
            local.wait()
            away.wait_recv()
        away.wait_send()


def gather(queries, keys, values, grads, total_blocks):
    anywhere = pl.BlockSpec(memory_space=pl.ANY)
    tokens = queries.shape[0]
    moved = jax.ShapeDtypeStruct((2 * tokens, GROUP * HD), jnp.bfloat16)
    dma = pltpu.SemaphoreType.DMA
    return pl.pallas_call(
        gather_kernel,
        in_specs=[anywhere] * 4,
        out_specs=[anywhere] * 3,
        out_shape=[moved, moved, jax.ShapeDtypeStruct((total_blocks * BLOCK, 2 * HD), jnp.bfloat16)],
        scratch_shapes=[
            dma((4,)), dma((4,)), dma((4,)), dma((LINE,)), dma((LINE,)), dma((LINE,)), dma((2 * LINE,)),
            dma((LINE,)), dma((LINE,)), dma((2 * LINE,)),
        ],
        compiler_params=pltpu.CompilerParams(collective_id=0, has_side_effects=True),
        name="gather",
    )(queries, keys, values, grads)


def reduce_kernel(
    grads, local, key_grad, value_grad,
    c_in, y_out, y_in, z_out, z_in, total, c_send, c_recv, y_send, y_recv, z_send, z_recv,
):
    z, y, c = place()

    def rows_of(zz, yy, cc):
        return pl.multiple_of(index_of(zz, yy, cc) * SHARD, SHARD)

    def beside(zz, yy):
        slot = zz * 2 + yy
        part = grads.at[pl.ds(rows_of(zz, yy, 1 - c), SHARD), :]
        return remote(part, c_in.at[slot], c_send.at[slot], c_recv.at[slot], ctx=index_of(z, y, 1 - c))

    def across(zz):
        return remote(y_out.at[zz], y_in.at[zz], y_send.at[zz], y_recv.at[zz], ctx=index_of(z, 1 - y, c))

    def up(zz):
        return remote(z_out.at[zz], z_in.at[0, zz], z_send.at[zz], z_recv.at[0, zz], ctx=index_of((z + 1) % LINE, y, c))

    def down(zz):
        return remote(z_out.at[zz], z_in.at[1, zz], z_send.at[zz], z_recv.at[1, zz], ctx=index_of((z + 3) % LINE, y, c))

    def pick(options):
        return jnp.where(z == 0, options[0], jnp.where(z == 1, options[1], jnp.where(z == 2, options[2], options[3])))

    order = [pick(options) for options in ((3, 3, 0, 0), (2, 0, 3, 1), (1, 2, 1, 2))] + [z]

    greet(z, y, c, None)
    for zz in order:
        beside(zz, 1 - y).start()
    for zz in order:
        beside(zz, y).start()

    def tiles(body):
        @pl.loop(0, QB_DEV)
        def _(i):
            body(pl.multiple_of(i * BLOCK, BLOCK))

    for zz in order:
        beside(zz, 1 - y).wait_recv()
        base = rows_of(zz, 1 - y, c)

        def fold(row, zz=zz, base=base):
            mine = grads[pl.ds(base + row, BLOCK), :].astype(jnp.float32)
            theirs = c_in[zz * 2 + 1 - y, pl.ds(row, BLOCK), :].astype(jnp.float32)
            y_out[zz, pl.ds(row, BLOCK), :] = (mine + theirs).astype(jnp.bfloat16)

        tiles(fold)
        across(zz).start()

    for zz in order[:3]:
        beside(zz, y).wait_recv()
        across(zz).wait_recv()
        base = rows_of(zz, y, c)

        def gathered(row, zz=zz, base=base):
            mine = grads[pl.ds(base + row, BLOCK), :].astype(jnp.float32)
            theirs = c_in[zz * 2 + y, pl.ds(row, BLOCK), :].astype(jnp.float32)
            return mine + theirs + y_in[zz, pl.ds(row, BLOCK), :].astype(jnp.float32)

        def start(row):
            z_out[zz, pl.ds(row, BLOCK), :] = gathered(row).astype(jnp.bfloat16)

        def extend(side):
            def body(row):
                part = z_in[side, zz, pl.ds(row, BLOCK), :].astype(jnp.float32)
                z_out[zz, pl.ds(row, BLOCK), :] = (gathered(row) + part).astype(jnp.bfloat16)

            return body

        @pl.when((z == 0) | (z == LINE - 1))
        def _():
            tiles(start)

        @pl.when((z > 0) & (z < LINE - 1) & (zz > z))
        def _():
            up(zz).wait_recv()
            tiles(extend(0))

        @pl.when((z > 0) & (z < LINE - 1) & (zz < z))
        def _():
            down(zz).wait_recv()
            tiles(extend(1))

        @pl.when(zz > z)
        def _():
            up(zz).start()

        @pl.when(zz < z)
        def _():
            down(zz).start()

    beside(z, y).wait_recv()
    across(z).wait_recv()

    def own(row):
        rows = pl.ds(row, BLOCK)
        theirs = c_in[z * 2 + y, rows, :].astype(jnp.float32)
        total[rows, :] = local[rows, :] + theirs + y_in[z, rows, :].astype(jnp.float32)

    def add(side):
        def body(row):
            rows = pl.ds(row, BLOCK)
            total[rows, :] += z_in[side, z, rows, :].astype(jnp.float32)

        return body

    tiles(own)

    @pl.when(z > 0)
    def _():
        up(z).wait_recv()
        tiles(add(0))

    @pl.when(z < LINE - 1)
    def _():
        down(z).wait_recv()
        tiles(add(1))

    key_grad[...] = total[:, :HD].astype(jnp.bfloat16)
    value_grad[...] = total[:, HD:].astype(jnp.bfloat16)

    for zz in range(LINE):
        beside(zz, 0).wait_send()
        beside(zz, 1).wait_send()
        across(zz).wait_send()

        @pl.when(zz != z)
        def _():
            up(zz).wait_send()


def reduce(grads, local):
    in_vmem = pl.BlockSpec(memory_space=pltpu.VMEM)
    dma = pltpu.SemaphoreType.DMA
    part = (SHARD, 2 * HD)
    result = jax.ShapeDtypeStruct((SHARD, HD), jnp.bfloat16)
    return pl.pallas_call(
        reduce_kernel,
        in_specs=[in_vmem] * 2,
        out_specs=[in_vmem] * 2,
        out_shape=[result, result],
        scratch_shapes=[
            pltpu.VMEM((2 * LINE, *part), jnp.bfloat16),
            pltpu.VMEM((LINE, *part), jnp.bfloat16),
            pltpu.VMEM((LINE, *part), jnp.bfloat16),
            pltpu.VMEM((LINE, *part), jnp.bfloat16),
            pltpu.VMEM((2, LINE, *part), jnp.bfloat16),
            pltpu.VMEM(part, jnp.float32),
            dma((2 * LINE,)), dma((2 * LINE,)), dma((LINE,)), dma((LINE,)), dma((LINE,)), dma((2, LINE)),
        ],
        compiler_params=pltpu.CompilerParams(
            collective_id=1, has_side_effects=True, vmem_limit_bytes=48 << 20
        ),
        name="reduce",
    )(grads, local)


def body_line(queries, keys, values, out_grad, rand_blocks, rand_count):
    total_blocks = rand_blocks.shape[0]
    head_queries, head_grads, pool = gather(queries, keys, values, out_grad, total_blocks)
    pool = pool.reshape(total_blocks, BLOCK, 2 * HD)
    query_grad, local_grads, all_grads = attend(
        rand_blocks, rand_count, head_queries, head_grads, pool, direct=True
    )
    key_grad, value_grad = reduce(
        all_grads.reshape(total_blocks * BLOCK, 2 * HD), local_grads.reshape(SHARD, 2 * HD)
    )
    return (query_grad, key_grad, value_grad)


def solution(mesh):
    line = mesh.shape["ctx"] == 4 * LINE and mesh.shape["head"] == 2
    placed = P(("ctx", "head"), None)
    return jax.shard_map(
        body_line if line else body,
        mesh=mesh,
        in_specs=(placed, placed, placed, placed, P(), P()),
        out_specs=(P("ctx", "head"), P("ctx", "head"), P("ctx", "head")),
        check_vma=False,
    )
```

```python
import functools
import math

import jax
import jax.numpy as jnp
from jax import lax
from jax.experimental import pallas as pl
from jax.experimental.pallas import tpu as pltpu
from jax.sharding import PartitionSpec as P

BLOCK = 128
HD = 128
GROUP = 4
G = 2
RAND = 3
QB_DEV = 6
NKB = 8
FACTOR = 1.0 / math.sqrt(HD)
EXP_FACTOR = FACTOR * math.log2(math.e)
CONTRACT_LAST = (((1,), (1,)), ((), ()))
CONTRACT_FIRST = (((0,), (0,)), ((), ()))
CONTRACT_MATMUL = (((1,), (0,)), ((), ()))


def dot(a, b, dims=CONTRACT_MATMUL):
    return lax.dot_general(a, b, dims, preferred_element_type=jnp.float32)


def attend_kernel(
    direct, table, valid, query_ref, grad_ref, pool_ref,
    dquery_ref, local_ref, far_ref, total, scores, dprobs, dscores, keys,
):
    step = pl.program_id(0)
    per_dev = local_ref.shape[0]
    first = 0
    if direct:
        first = lax.axis_index("ctx") * per_dev
        block = first + step
        last = pool_ref.shape[0] - 1
        entry = [jnp.maximum(block - 1, 0), block, jnp.minimum(block + 1, last), 0, 1]
        entry += [table[block, r] for r in range(RAND)]
        use = [block > 0, True, block < last, True, True]
        use += [r < valid[block] for r in range(RAND)]
    else:
        entry = [table[step, e] for e in range(NKB)]
        use = [valid[step, e] > 0 for e in range(NKB)]

    @pl.when(step == 0)
    def _():
        total[...] = jnp.zeros_like(total)

    query = jnp.concatenate([query_ref[:, h * HD : (h + 1) * HD] for h in range(GROUP)], axis=0)
    grad = jnp.concatenate([grad_ref[:, h * HD : (h + 1) * HD] for h in range(GROUP)], axis=0)
    rows = [slice(e * BLOCK, (e + 1) * BLOCK) for e in range(NKB)]
    row_max = None
    for e in range(NKB):
        key_tile = pool_ref[entry[e], :, :HD]
        keys[rows[e], :] = key_tile
        tile = dot(key_tile, query, CONTRACT_LAST)
        if use[e] is not True:
            tile += jnp.where(use[e], 0.0, -jnp.inf).astype(jnp.float32)
        scores[rows[e], :] = tile
        tile_max = jnp.max(tile, axis=0, keepdims=True)
        row_max = tile_max if e == 0 else jnp.maximum(row_max, tile_max)
    row_sum = jnp.zeros_like(row_max)
    row_dot = jnp.zeros_like(row_max)
    for e in range(NKB):
        weight = jnp.exp2((scores[rows[e], :] - row_max) * EXP_FACTOR)
        dprob = dot(pool_ref[entry[e], :, HD:], grad, CONTRACT_LAST)
        row_sum += jnp.sum(weight, axis=0, keepdims=True)
        row_dot += jnp.sum(weight * dprob, axis=0, keepdims=True)
        scores[rows[e], :] = weight
        dprobs[rows[e], :] = dprob
    scale = 1.0 / row_sum
    row_dot = row_dot * scale
    for e in range(NKB):
        weight = scores[rows[e], :] * scale
        dscore = (weight * (dprobs[rows[e], :] - row_dot)).astype(jnp.bfloat16)
        dscores[rows[e], :] = dscore
        total[entry[e], :, :HD] += dot(dscore, query) * FACTOR
        total[entry[e], :, HD:] += dot(weight.astype(jnp.bfloat16), grad)
    dquery = dot(keys[...], dscores[...], CONTRACT_FIRST) * FACTOR
    for h in range(GROUP):
        dquery_ref[:, h * HD : (h + 1) * HD] = dquery[:, h * BLOCK : (h + 1) * BLOCK].T.astype(
            jnp.bfloat16
        )

    @pl.when(step == pl.num_programs(0) - 1)
    def _():
        local_ref[...] = total[pl.ds(first, per_dev)]
        skip = total.shape[0] - far_ref.shape[0]

        @pl.loop(0, far_ref.shape[0])
        def _(i):
            far_ref[i] = total[skip + i].astype(jnp.bfloat16)


def attend(table, valid, queries, grads, pool, direct=False):
    pool_size = pool.shape[0]
    per_dev = QB_DEV
    far_size = pool_size if direct else pool_size - per_dev
    tile = pl.BlockSpec((BLOCK, GROUP * HD), lambda i, *_: (i, 0))
    whole = lambda size: pl.BlockSpec((size, BLOCK, 2 * HD), lambda i, *_: (0, 0, 0), pipeline_mode=pl.Buffered(1))
    return pl.pallas_call(
        functools.partial(attend_kernel, direct),
        grid_spec=pltpu.PrefetchScalarGridSpec(
            num_scalar_prefetch=2,
            grid=(per_dev,),
            in_specs=[tile, tile, whole(pool_size)],
            out_specs=[tile, whole(per_dev), whole(far_size)],
            scratch_shapes=[
                pltpu.VMEM((pool_size, BLOCK, 2 * HD), jnp.float32),
                pltpu.VMEM((NKB * BLOCK, GROUP * BLOCK), jnp.float32),
                pltpu.VMEM((NKB * BLOCK, GROUP * BLOCK), jnp.float32),
                pltpu.VMEM((NKB * BLOCK, GROUP * BLOCK), jnp.bfloat16),
                pltpu.VMEM((NKB * BLOCK, HD), jnp.bfloat16),
            ],
        ),
        out_shape=[
            jax.ShapeDtypeStruct(queries.shape, jnp.bfloat16),
            jax.ShapeDtypeStruct((per_dev, BLOCK, 2 * HD), jnp.float32),
            jax.ShapeDtypeStruct((far_size, BLOCK, 2 * HD), jnp.bfloat16),
        ],
        compiler_params=pltpu.CompilerParams(vmem_limit_bytes=62 << 20),
        name="attend",
    )(table, valid, queries, grads, pool)


def exchange(array):
    return lax.all_to_all(array, "ctx", split_axis=0, concat_axis=0, tiled=True)


def body(queries, keys, values, out_grad, rand_blocks, rand_count):
    heads = lax.axis_size("head")
    shards = lax.axis_size("ctx")
    myself = lax.axis_index("ctx")
    per_dev = QB_DEV
    entries = per_dev * RAND
    owners_used = min(entries, shards - 3)
    capacity = (entries + owners_used - 1) // owners_used
    total_blocks = per_dev * shards
    far_slots = shards * capacity
    piece = G * BLOCK // shards

    tokens = keys.shape[0]
    pairs = jnp.stack([keys.reshape(tokens, heads, HD), values.reshape(tokens, heads, HD)], axis=2)
    pairs = pairs.transpose(1, 0, 2, 3).reshape(heads, tokens, 2 * HD)
    local_rows = lax.all_to_all(pairs, "head", split_axis=0, concat_axis=0, tiled=True)
    local_rows = local_rows.reshape(heads * tokens, 2 * HD)
    local_pairs = local_rows.reshape(per_dev, BLOCK, 2 * HD)
    head_queries = lax.all_to_all(queries, "head", split_axis=1, concat_axis=0, tiled=True)
    head_grads = lax.all_to_all(out_grad, "head", split_axis=1, concat_axis=0, tiled=True)

    flat_blocks = rand_blocks.reshape(shards, entries)
    owners = flat_blocks // per_dev
    offsets = flat_blocks % per_dev
    positions = jnp.arange(entries, dtype=jnp.int32)
    earlier = positions[None, :] < positions[:, None]
    same_owner = owners[:, :, None] == owners[:, None, :]
    slot_ranks = jnp.sum(same_owner & earlier[None], axis=2)
    slot_range = jnp.arange(capacity, dtype=jnp.int32)
    send_hits = (
        (owners == myself)[:, None, :] & (slot_ranks[:, None, :] == slot_range[None, :, None])
    ).astype(jnp.float32)
    offset_hot = (
        offsets[:, :, None] == jnp.arange(per_dev, dtype=jnp.int32)[None, None, :]
    ).astype(jnp.float32)
    send_table = jnp.einsum("dme,deq->dmq", send_hits, offset_hot)
    targets = jnp.arange(shards, dtype=jnp.int32)[:, None, None]
    first_slot = (slot_range == 0)[None, :, None]
    block_range = jnp.arange(per_dev, dtype=jnp.int32)[None, None, :]
    right_send = (targets == (myself + 1) % shards) & first_slot & (block_range == per_dev - 1)
    left_send = (targets == (myself - 1 + shards) % shards) & first_slot & (block_range == 0)
    send_table = send_table + right_send.astype(jnp.float32) + left_send.astype(jnp.float32)
    left_far = per_dev + (myself - 1 + shards) % shards * capacity
    right_far = per_dev + (myself + 1) % shards * capacity
    outgoing = jnp.einsum(
        "dmq,qtc->dmtc",
        send_table.astype(jnp.bfloat16),
        local_pairs,
        preferred_element_type=jnp.float32,
    ).astype(jnp.bfloat16)
    pieces = local_rows[: G * BLOCK].reshape(shards, piece, 2 * HD)
    packed = jnp.concatenate([outgoing.reshape(shards, capacity * BLOCK, 2 * HD), pieces], axis=1)
    arrived = exchange(packed)
    far_pairs = arrived[:, : capacity * BLOCK].reshape(far_slots, BLOCK, 2 * HD)
    my_piece = jnp.broadcast_to(arrived[0, capacity * BLOCK :][None], (shards, piece, 2 * HD))
    global_pairs = exchange(my_piece).reshape(G, BLOCK, 2 * HD)
    pool = jnp.concatenate([local_pairs, far_pairs, global_pairs], axis=0)

    edge_base = per_dev + far_slots
    local_index = jnp.arange(per_dev, dtype=jnp.int32)
    seq_block = myself * per_dev + local_index
    left_index = jnp.where(local_index > 0, local_index - 1, left_far)
    right_index = jnp.where(local_index < per_dev - 1, local_index + 1, right_far)
    global_index = jnp.broadcast_to(
        edge_base + jnp.arange(G, dtype=jnp.int32)[None, :], (per_dev, G)
    )
    my_owners = lax.dynamic_index_in_dim(owners, myself, 0, keepdims=False)
    my_ranks = lax.dynamic_index_in_dim(slot_ranks, myself, 0, keepdims=False)
    random_index = (per_dev + my_owners * capacity + my_ranks).reshape(per_dev, RAND)
    key_table = jnp.concatenate(
        [jnp.stack([left_index, local_index, right_index], axis=1), global_index, random_index],
        axis=1,
    ).astype(jnp.int32)
    my_counts = lax.dynamic_slice_in_dim(rand_count, myself * per_dev, per_dev)
    key_valid = jnp.concatenate(
        [
            jnp.stack([seq_block > 0, seq_block >= 0, seq_block < total_blocks - 1], axis=1),
            jnp.ones((per_dev, G), bool),
            jnp.arange(RAND, dtype=jnp.int32)[None, :] < my_counts[:, None],
        ],
        axis=1,
    ).astype(jnp.int32)

    query_grad, local_grads, far_grads = attend(key_table, key_valid, head_queries, head_grads, pool)

    packed_grads = jnp.concatenate(
        [
            far_grads[:far_slots].reshape(shards, capacity * BLOCK, 2 * HD),
            far_grads[far_slots:].reshape(shards, piece, 2 * HD),
        ],
        axis=1,
    )
    returned = exchange(packed_grads)
    returned_far = returned[:, : capacity * BLOCK].reshape(shards, capacity, BLOCK, 2 * HD)
    global_piece = jnp.sum(returned[:, capacity * BLOCK :].astype(jnp.float32), axis=0)
    global_piece = jnp.broadcast_to(global_piece[None].astype(jnp.bfloat16), (shards, piece, 2 * HD))
    global_total = exchange(global_piece).reshape(G, BLOCK, 2 * HD).astype(jnp.float32)
    local_grads = local_grads + jnp.einsum(
        "dmq,dmtc->qtc",
        send_table.astype(jnp.bfloat16),
        returned_far,
        preferred_element_type=jnp.float32,
    )
    local_grads = local_grads.at[:G].add(
        jnp.where(myself == 0, global_total, jnp.zeros_like(global_total))
    )
    key_grad = local_grads[:, :, :HD].reshape(per_dev * BLOCK, HD).astype(jnp.bfloat16)
    value_grad = local_grads[:, :, HD:].reshape(per_dev * BLOCK, HD).astype(jnp.bfloat16)
    return (query_grad, key_grad, value_grad)

MESH = pl.DeviceIdType.MESH
LINE = 4
SHARD = QB_DEV * BLOCK


def place():
    me = lax.axis_index("ctx")
    return me // 4, (me // 2) % 2, me % 2


def index_of(z, y, c):
    return z * 4 + y * 2 + c


def remote(src, dst, send_sem, recv_sem, **device):
    return pltpu.make_async_remote_copy(
        src_ref=src, dst_ref=dst, send_sem=send_sem, recv_sem=recv_sem, device_id=device, device_id_type=MESH
    )


def greet(z, y, c, head):
    barrier = pltpu.get_barrier_semaphore()

    def tell(**device):
        pl.semaphore_signal(barrier, inc=1, device_id=device, device_id_type=MESH)

    tell(ctx=index_of(z, 1 - y, c))
    tell(ctx=index_of(z, y, 1 - c))
    if head is not None:
        tell(head=1 - head)

    @pl.when(z > 0)
    def _():
        tell(ctx=index_of(z - 1, y, c))

    @pl.when(z < LINE - 1)
    def _():
        tell(ctx=index_of(z + 1, y, c))

    peers = (2 if head is None else 3) + (z + 2) // 3 + (5 - z) // 3
    pl.semaphore_wait(barrier, peers)


def gather_kernel(
    q_in, k_in, v_in, g_in, q_out, g_out, pool,
    local_sem, head_send, head_recv, up_send, down_send, y_send, c_send, z_recv, y_recv, c_recv,
):
    z, y, c = place()
    me = index_of(z, y, c)
    head = lax.axis_index("head")
    other = 1 - head
    tokens = k_in.shape[0]

    def half(zz, yy, u):
        start = index_of(zz, yy, c) * SHARD + u * tokens
        return pool.at[pl.ds(pl.multiple_of(start, tokens), tokens), :]

    pool_rows = pl.ds(pl.multiple_of(me * SHARD + head * tokens, tokens), tokens)
    out_rows = pl.ds(pl.multiple_of(head * tokens, tokens), tokens)
    jobs = []
    for src, dst, width in (
        (k_in, pool.at[pool_rows, :HD], HD),
        (v_in, pool.at[pool_rows, HD:], HD),
        (q_in, q_out.at[out_rows, :], GROUP * HD),
        (g_in, g_out.at[out_rows, :], GROUP * HD),
    ):
        i = len(jobs)
        mine = src.at[:, pl.ds(pl.multiple_of(head * width, width), width)]
        theirs = src.at[:, pl.ds(pl.multiple_of(other * width, width), width)]
        jobs.append(
            (
                pltpu.make_async_copy(mine, dst, local_sem.at[i]),
                remote(theirs, dst, head_send.at[i], head_recv.at[i], head=other),
            )
        )
    for local, _ in jobs:
        local.start()
    greet(z, y, c, head)
    for _, away in jobs[:2]:
        away.start()

    def up(zz, u):
        part = half(zz, y, u)
        slot = zz * 2 + u
        return remote(part, part, up_send.at[slot], z_recv.at[slot], ctx=index_of((z + 1) % LINE, y, c))

    def down(zz, u):
        part = half(zz, y, u)
        slot = zz * 2 + u
        return remote(part, part, down_send.at[slot], z_recv.at[slot], ctx=index_of((z + 3) % LINE, y, c))

    def across(zz, u):
        part = half(zz, y, u)
        slot = zz * 2 + u
        return remote(part, part, y_send.at[slot], y_recv.at[slot], ctx=index_of(z, 1 - y, c))

    def beside(zz, yy, u):
        part = half(zz, yy, u)
        slot = zz * 4 + yy * 2 + u
        return remote(part, part, c_send.at[slot], c_recv.at[slot], ctx=index_of(z, y, 1 - c))

    def pass_on(zz, u, upward, downward):
        if upward:

            @pl.when(z < LINE - 1)
            def _():
                up(zz, u).start()

        if downward:

            @pl.when(z > 0)
            def _():
                down(zz, u).start()

        across(zz, u).start()
        beside(zz, y, u).start()

    for local, _ in jobs[:2]:
        local.wait()
    pass_on(z, head, True, True)
    for _, away in jobs[:2]:
        away.wait_recv()
    pass_on(z, other, True, True)
    for _, away in jobs[2:]:
        away.start()

    def from_partner(zz, u):
        across(zz, u).wait_recv()
        beside(zz, 1 - y, u).start()

    def from_below(zz, u):
        up(zz, u).wait_recv()
        pass_on(zz, u, True, False)

    def from_above(zz, u):
        down(zz, u).wait_recv()
        pass_on(zz, u, False, True)

    def stage(j, u, below, above):
        @pl.when(z - j >= 0)
        def _():
            below(z - j, u)

        @pl.when(z + j <= LINE - 1)
        def _():
            above(z + j, u)

    for j in range(1, LINE):
        for u in (head, other):
            stage(j, u, from_below, from_above)
            if j == 1:
                from_partner(z, u)
            else:
                stage(j - 1, u, from_partner, from_partner)
    for u in (head, other):
        stage(LINE - 1, u, from_partner, from_partner)

    for zz in range(LINE):
        for u in range(2):
            for yy in range(2):
                beside(zz, yy, u).wait_recv()
                beside(zz, yy, u).wait_send()
            across(zz, u).wait_send()

            @pl.when((z < LINE - 1) & (zz <= z))
            def _():
                up(zz, u).wait_send()

            @pl.when((z > 0) & (zz >= z))
            def _():
                down(zz, u).wait_send()

    for i, (local, away) in enumerate(jobs):
        if i >= 2:
            local.wait()
            away.wait_recv()
        away.wait_send()


def gather(queries, keys, values, grads, total_blocks):
    anywhere = pl.BlockSpec(memory_space=pl.ANY)
    tokens = queries.shape[0]
    moved = jax.ShapeDtypeStruct((2 * tokens, GROUP * HD), jnp.bfloat16)
    dma = pltpu.SemaphoreType.DMA
    return pl.pallas_call(
        gather_kernel,
        in_specs=[anywhere] * 4,
        out_specs=[anywhere] * 3,
        out_shape=[moved, moved, jax.ShapeDtypeStruct((total_blocks * BLOCK, 2 * HD), jnp.bfloat16)],
        scratch_shapes=[
            dma((4,)), dma((4,)), dma((4,)), dma((2 * LINE,)), dma((2 * LINE,)), dma((2 * LINE,)), dma((4 * LINE,)),
            dma((2 * LINE,)), dma((2 * LINE,)), dma((4 * LINE,)),
        ],
        compiler_params=pltpu.CompilerParams(collective_id=0, has_side_effects=True),
        name="gather",
    )(queries, keys, values, grads)


def reduce_kernel(
    grads, local, key_grad, value_grad,
    c_in, y_out, y_in, z_out, z_in, c_send, c_recv, y_send, y_recv, z_send, z_recv,
):
    z, y, c = place()

    size = SHARD // 2

    def rows_of(zz, yy, cc, u):
        return pl.multiple_of(index_of(zz, yy, cc) * SHARD + u * size, size)

    def beside(zz, yy, u):
        slot = zz * 4 + yy * 2 + u
        part = grads.at[pl.ds(rows_of(zz, yy, 1 - c, u), size), :]
        return remote(part, c_in.at[slot], c_send.at[slot], c_recv.at[slot], ctx=index_of(z, y, 1 - c))

    def across(zz, u):
        slot = zz * 2 + u
        return remote(
            y_out.at[slot], y_in.at[slot], y_send.at[slot], y_recv.at[slot], ctx=index_of(z, 1 - y, c)
        )

    def up(zz, u):
        slot = zz * 2 + u
        return remote(
            z_out.at[slot], z_in.at[0, slot], z_send.at[slot], z_recv.at[0, slot],
            ctx=index_of((z + 1) % LINE, y, c),
        )

    def down(zz, u):
        slot = zz * 2 + u
        return remote(
            z_out.at[slot], z_in.at[1, slot], z_send.at[slot], z_recv.at[1, slot],
            ctx=index_of((z + 3) % LINE, y, c),
        )

    def pick(options):
        return jnp.where(z == 0, options[0], jnp.where(z == 1, options[1], jnp.where(z == 2, options[2], options[3])))

    order = [pick(options) for options in ((3, 3, 0, 0), (2, 0, 3, 1), (1, 2, 1, 2))] + [z]
    units = [(zz, u) for zz in order for u in range(2)]

    def send_beside(i):
        if i < len(units):
            beside(units[i][0], 1 - y, units[i][1]).start()
            beside(units[i][0], y, units[i][1]).start()

    def tiles(body):
        @pl.loop(0, size // BLOCK)
        def _(i):
            body(pl.multiple_of(i * BLOCK, BLOCK))

    def fold_across(i):
        zz, u = units[i]
        beside(zz, 1 - y, u).wait_recv()
        base = rows_of(zz, 1 - y, c, u)

        def fold(row):
            mine = grads[pl.ds(base + row, BLOCK), :].astype(jnp.float32)
            theirs = c_in[zz * 4 + (1 - y) * 2 + u, pl.ds(row, BLOCK), :].astype(jnp.float32)
            y_out[zz * 2 + u, pl.ds(row, BLOCK), :] = (mine + theirs).astype(jnp.bfloat16)

        tiles(fold)
        if i >= 2:
            across(*units[i - 2]).wait_send()
        across(zz, u).start()

    def along(i):
        zz, u = units[i]
        slot = zz * 2 + u
        beside(zz, y, u).wait_recv()
        across(zz, u).wait_recv()
        base = rows_of(zz, y, c, u)

        def gathered(row, mine):
            theirs = c_in[zz * 4 + y * 2 + u, pl.ds(row, BLOCK), :].astype(jnp.float32)
            return mine + theirs + y_in[slot, pl.ds(row, BLOCK), :].astype(jnp.float32)

        def part(side, row):
            return z_in[side, slot, pl.ds(row, BLOCK), :].astype(jnp.float32)

        if i >= len(units) - 2:
            own = pl.multiple_of(u * size, size)

            def finish(*sides):
                def body(row):
                    rows = pl.ds(own + row, BLOCK)
                    total = gathered(row, local[rows, :])
                    for side in sides:
                        total += part(side, row)
                    key_grad[rows, :] = total[:, :HD].astype(jnp.bfloat16)
                    value_grad[rows, :] = total[:, HD:].astype(jnp.bfloat16)

                tiles(body)

            @pl.when(z == 0)
            def _():
                down(zz, u).wait_recv()
                finish(1)

            @pl.when(z == LINE - 1)
            def _():
                up(zz, u).wait_recv()
                finish(0)

            @pl.when((z > 0) & (z < LINE - 1))
            def _():
                up(zz, u).wait_recv()
                down(zz, u).wait_recv()
                finish(0, 1)

            return

        def extend(*sides):
            def body(row):
                total = gathered(row, grads[pl.ds(base + row, BLOCK), :].astype(jnp.float32))
                for side in sides:
                    total += part(side, row)
                z_out[slot, pl.ds(row, BLOCK), :] = total.astype(jnp.bfloat16)

            tiles(body)

        @pl.when((z == 0) | (z == LINE - 1))
        def _():
            extend()

        @pl.when((z > 0) & (z < LINE - 1) & (zz > z))
        def _():
            up(zz, u).wait_recv()
            extend(0)

        @pl.when((z > 0) & (z < LINE - 1) & (zz < z))
        def _():
            down(zz, u).wait_recv()
            extend(1)

        @pl.when(zz > z)
        def _():
            up(zz, u).start()

        @pl.when(zz < z)
        def _():
            down(zz, u).start()

    greet(z, y, c, None)
    send_beside(0)
    send_beside(1)
    for i in range(len(units) + 2):
        if i < len(units):
            fold_across(i)
            send_beside(i + 2)
        if i >= 2:
            along(i - 2)

    for i, (zz, u) in enumerate(units):
        beside(zz, 0, u).wait_send()
        beside(zz, 1, u).wait_send()
        if i >= len(units) - 2:
            across(zz, u).wait_send()
        else:
            up(zz, u).wait_send()


def reduce(grads, local):
    in_vmem = pl.BlockSpec(memory_space=pltpu.VMEM)
    dma = pltpu.SemaphoreType.DMA
    part = (SHARD // 2, 2 * HD)
    result = jax.ShapeDtypeStruct((SHARD, HD), jnp.bfloat16)
    return pl.pallas_call(
        reduce_kernel,
        in_specs=[in_vmem] * 2,
        out_specs=[in_vmem] * 2,
        out_shape=[result, result],
        scratch_shapes=[
            pltpu.VMEM((4 * LINE, *part), jnp.bfloat16),
            pltpu.VMEM((2 * LINE, *part), jnp.bfloat16),
            pltpu.VMEM((2 * LINE, *part), jnp.bfloat16),
            pltpu.VMEM((2 * LINE, *part), jnp.bfloat16),
            pltpu.VMEM((2, 2 * LINE, *part), jnp.bfloat16),
            dma((4 * LINE,)), dma((4 * LINE,)), dma((2 * LINE,)), dma((2 * LINE,)), dma((2 * LINE,)), dma((2, 2 * LINE)),
        ],
        compiler_params=pltpu.CompilerParams(
            collective_id=1, has_side_effects=True, vmem_limit_bytes=48 << 20
        ),
        name="reduce",
    )(grads, local)


def body_line(queries, keys, values, out_grad, rand_blocks, rand_count):
    total_blocks = rand_blocks.shape[0]
    head_queries, head_grads, pool = gather(queries, keys, values, out_grad, total_blocks)
    pool = pool.reshape(total_blocks, BLOCK, 2 * HD)
    query_grad, local_grads, all_grads = attend(
        rand_blocks, rand_count, head_queries, head_grads, pool, direct=True
    )
    key_grad, value_grad = reduce(
        all_grads.reshape(total_blocks * BLOCK, 2 * HD), local_grads.reshape(SHARD, 2 * HD)
    )
    return (query_grad, key_grad, value_grad)


def solution(mesh):
    line = mesh.shape["ctx"] == 4 * LINE and mesh.shape["head"] == 2
    placed = P(("ctx", "head"), None)
    return jax.shard_map(
        body_line if line else body,
        mesh=mesh,
        in_specs=(placed, placed, placed, placed, P(), P()),
        out_specs=(P("ctx", "head"), P("ctx", "head"), P("ctx", "head")),
        check_vma=False,
    )
```

```python
import functools
import math

import jax
import jax.numpy as jnp
from jax import lax
from jax.experimental import pallas as pl
from jax.experimental.pallas import tpu as pltpu
from jax.sharding import PartitionSpec as P

BLOCK = 128
HD = 128
GROUP = 4
G = 2
RAND = 3
QB_DEV = 6
NKB = 8
FACTOR = 1.0 / math.sqrt(HD)
EXP_FACTOR = FACTOR * math.log2(math.e)
CONTRACT_LAST = (((1,), (1,)), ((), ()))
CONTRACT_FIRST = (((0,), (0,)), ((), ()))
CONTRACT_MATMUL = (((1,), (0,)), ((), ()))


def dot(a, b, dims=CONTRACT_MATMUL):
    return lax.dot_general(a, b, dims, preferred_element_type=jnp.float32)


def attend_kernel(
    direct, table, valid, query_ref, grad_ref, pool_hbm,
    dquery_ref, local_ref, far_ref, total, scores, dprobs, dscores, keys, held, sems,
):
    step = pl.program_id(0)
    per_dev = local_ref.shape[0]
    first = 0
    if direct:
        first = lax.axis_index("ctx") * per_dev
        block = first + step
        last = held.shape[0] - 1
        entry = [jnp.maximum(block - 1, 0), block, jnp.minimum(block + 1, last), 0, 1]
        entry += [table[r, block] for r in range(RAND)]
        use = [block > 0, True, block < last, True, True]
        use += [r < valid[block] for r in range(RAND)]
    else:
        entry = [table[step, e] for e in range(NKB)]
        use = [valid[step, e] > 0 for e in range(NKB)]

    @pl.when(step == 0)
    def _():
        load = pltpu.make_async_copy(pool_hbm, held, sems.at[0])
        load.start()
        total[...] = jnp.zeros_like(total)
        load.wait()

    query = jnp.concatenate([query_ref[:, h * HD : (h + 1) * HD] for h in range(GROUP)], axis=0)
    grad = jnp.concatenate([grad_ref[:, h * HD : (h + 1) * HD] for h in range(GROUP)], axis=0)
    rows = [slice(e * BLOCK, (e + 1) * BLOCK) for e in range(NKB)]
    row_max = None
    for e in range(NKB):
        key_tile = held[entry[e], :, :HD]
        keys[rows[e], :] = key_tile
        tile = dot(key_tile, query, CONTRACT_LAST)
        if use[e] is not True:
            tile += jnp.where(use[e], 0.0, -jnp.inf).astype(jnp.float32)
        scores[rows[e], :] = tile
        tile_max = jnp.max(tile, axis=0, keepdims=True)
        row_max = tile_max if e == 0 else jnp.maximum(row_max, tile_max)
    row_sum = jnp.zeros_like(row_max)
    row_dot = jnp.zeros_like(row_max)
    for e in range(NKB):
        weight = jnp.exp2((scores[rows[e], :] - row_max) * EXP_FACTOR)
        dprob = dot(held[entry[e], :, HD:], grad, CONTRACT_LAST)
        row_sum += jnp.sum(weight, axis=0, keepdims=True)
        row_dot += jnp.sum(weight * dprob, axis=0, keepdims=True)
        scores[rows[e], :] = weight
        dprobs[rows[e], :] = dprob
    scale = 1.0 / row_sum
    row_dot = row_dot * scale
    for e in range(NKB):
        weight = scores[rows[e], :] * scale
        dscore = (weight * (dprobs[rows[e], :] - row_dot)).astype(jnp.bfloat16)
        dscores[rows[e], :] = dscore
        total[entry[e], :, :HD] += dot(dscore, query) * FACTOR
        total[entry[e], :, HD:] += dot(weight.astype(jnp.bfloat16), grad)
    dquery = dot(keys[...], dscores[...], CONTRACT_FIRST) * FACTOR
    for h in range(GROUP):
        dquery_ref[:, h * HD : (h + 1) * HD] = dquery[:, h * BLOCK : (h + 1) * BLOCK].T.astype(
            jnp.bfloat16
        )

    @pl.when(step == pl.num_programs(0) - 1)
    def _():
        local_ref[...] = total[pl.ds(first, per_dev)]
        skip = total.shape[0] - far_ref.shape[0]

        @pl.loop(0, far_ref.shape[0])
        def _(i):
            held[i] = total[skip + i].astype(jnp.bfloat16)
            pltpu.make_async_copy(held.at[i], far_ref.at[i], sems.at[1]).start()

        pltpu.make_async_copy(held.at[pl.ds(0, far_ref.shape[0])], far_ref, sems.at[1]).wait()


def attend(table, valid, queries, grads, pool, direct=False):
    pool_size = pool.shape[0]
    per_dev = QB_DEV
    far_size = pool_size if direct else pool_size - per_dev
    anywhere = pl.BlockSpec(memory_space=pl.ANY)
    tile = pl.BlockSpec((BLOCK, GROUP * HD), lambda i, *_: (i, 0))
    whole = lambda size: pl.BlockSpec((size, BLOCK, 2 * HD), lambda i, *_: (0, 0, 0), pipeline_mode=pl.Buffered(1))
    return pl.pallas_call(
        functools.partial(attend_kernel, direct),
        grid_spec=pltpu.PrefetchScalarGridSpec(
            num_scalar_prefetch=2,
            grid=(per_dev,),
            in_specs=[tile, tile, anywhere],
            out_specs=[tile, whole(per_dev), anywhere],
            scratch_shapes=[
                pltpu.VMEM((pool_size, BLOCK, 2 * HD), jnp.float32),
                pltpu.VMEM((NKB * BLOCK, GROUP * BLOCK), jnp.float32),
                pltpu.VMEM((NKB * BLOCK, GROUP * BLOCK), jnp.float32),
                pltpu.VMEM((NKB * BLOCK, GROUP * BLOCK), jnp.bfloat16),
                pltpu.VMEM((NKB * BLOCK, HD), jnp.bfloat16),
                pltpu.VMEM((pool_size, BLOCK, 2 * HD), jnp.bfloat16),
                pltpu.SemaphoreType.DMA((2,)),
            ],
        ),
        out_shape=[
            jax.ShapeDtypeStruct(queries.shape, jnp.bfloat16),
            jax.ShapeDtypeStruct((per_dev, BLOCK, 2 * HD), jnp.float32),
            jax.ShapeDtypeStruct((far_size, BLOCK, 2 * HD), jnp.bfloat16),
        ],
        compiler_params=pltpu.CompilerParams(vmem_limit_bytes=62 << 20),
        name="attend",
    )(table, valid, queries, grads, pool)


def exchange(array):
    return lax.all_to_all(array, "ctx", split_axis=0, concat_axis=0, tiled=True)


def body(queries, keys, values, out_grad, rand_blocks, rand_count):
    heads = lax.axis_size("head")
    shards = lax.axis_size("ctx")
    myself = lax.axis_index("ctx")
    per_dev = QB_DEV
    entries = per_dev * RAND
    owners_used = min(entries, shards - 3)
    capacity = (entries + owners_used - 1) // owners_used
    total_blocks = per_dev * shards
    far_slots = shards * capacity
    piece = G * BLOCK // shards

    tokens = keys.shape[0]
    pairs = jnp.stack([keys.reshape(tokens, heads, HD), values.reshape(tokens, heads, HD)], axis=2)
    pairs = pairs.transpose(1, 0, 2, 3).reshape(heads, tokens, 2 * HD)
    local_rows = lax.all_to_all(pairs, "head", split_axis=0, concat_axis=0, tiled=True)
    local_rows = local_rows.reshape(heads * tokens, 2 * HD)
    local_pairs = local_rows.reshape(per_dev, BLOCK, 2 * HD)
    head_queries = lax.all_to_all(queries, "head", split_axis=1, concat_axis=0, tiled=True)
    head_grads = lax.all_to_all(out_grad, "head", split_axis=1, concat_axis=0, tiled=True)

    flat_blocks = rand_blocks.reshape(shards, entries)
    owners = flat_blocks // per_dev
    offsets = flat_blocks % per_dev
    positions = jnp.arange(entries, dtype=jnp.int32)
    earlier = positions[None, :] < positions[:, None]
    same_owner = owners[:, :, None] == owners[:, None, :]
    slot_ranks = jnp.sum(same_owner & earlier[None], axis=2)
    slot_range = jnp.arange(capacity, dtype=jnp.int32)
    send_hits = (
        (owners == myself)[:, None, :] & (slot_ranks[:, None, :] == slot_range[None, :, None])
    ).astype(jnp.float32)
    offset_hot = (
        offsets[:, :, None] == jnp.arange(per_dev, dtype=jnp.int32)[None, None, :]
    ).astype(jnp.float32)
    send_table = jnp.einsum("dme,deq->dmq", send_hits, offset_hot)
    targets = jnp.arange(shards, dtype=jnp.int32)[:, None, None]
    first_slot = (slot_range == 0)[None, :, None]
    block_range = jnp.arange(per_dev, dtype=jnp.int32)[None, None, :]
    right_send = (targets == (myself + 1) % shards) & first_slot & (block_range == per_dev - 1)
    left_send = (targets == (myself - 1 + shards) % shards) & first_slot & (block_range == 0)
    send_table = send_table + right_send.astype(jnp.float32) + left_send.astype(jnp.float32)
    left_far = per_dev + (myself - 1 + shards) % shards * capacity
    right_far = per_dev + (myself + 1) % shards * capacity
    outgoing = jnp.einsum(
        "dmq,qtc->dmtc",
        send_table.astype(jnp.bfloat16),
        local_pairs,
        preferred_element_type=jnp.float32,
    ).astype(jnp.bfloat16)
    pieces = local_rows[: G * BLOCK].reshape(shards, piece, 2 * HD)
    packed = jnp.concatenate([outgoing.reshape(shards, capacity * BLOCK, 2 * HD), pieces], axis=1)
    arrived = exchange(packed)
    far_pairs = arrived[:, : capacity * BLOCK].reshape(far_slots, BLOCK, 2 * HD)
    my_piece = jnp.broadcast_to(arrived[0, capacity * BLOCK :][None], (shards, piece, 2 * HD))
    global_pairs = exchange(my_piece).reshape(G, BLOCK, 2 * HD)
    pool = jnp.concatenate([local_pairs, far_pairs, global_pairs], axis=0)

    edge_base = per_dev + far_slots
    local_index = jnp.arange(per_dev, dtype=jnp.int32)
    seq_block = myself * per_dev + local_index
    left_index = jnp.where(local_index > 0, local_index - 1, left_far)
    right_index = jnp.where(local_index < per_dev - 1, local_index + 1, right_far)
    global_index = jnp.broadcast_to(
        edge_base + jnp.arange(G, dtype=jnp.int32)[None, :], (per_dev, G)
    )
    my_owners = lax.dynamic_index_in_dim(owners, myself, 0, keepdims=False)
    my_ranks = lax.dynamic_index_in_dim(slot_ranks, myself, 0, keepdims=False)
    random_index = (per_dev + my_owners * capacity + my_ranks).reshape(per_dev, RAND)
    key_table = jnp.concatenate(
        [jnp.stack([left_index, local_index, right_index], axis=1), global_index, random_index],
        axis=1,
    ).astype(jnp.int32)
    my_counts = lax.dynamic_slice_in_dim(rand_count, myself * per_dev, per_dev)
    key_valid = jnp.concatenate(
        [
            jnp.stack([seq_block > 0, seq_block >= 0, seq_block < total_blocks - 1], axis=1),
            jnp.ones((per_dev, G), bool),
            jnp.arange(RAND, dtype=jnp.int32)[None, :] < my_counts[:, None],
        ],
        axis=1,
    ).astype(jnp.int32)

    query_grad, local_grads, far_grads = attend(key_table, key_valid, head_queries, head_grads, pool)

    packed_grads = jnp.concatenate(
        [
            far_grads[:far_slots].reshape(shards, capacity * BLOCK, 2 * HD),
            far_grads[far_slots:].reshape(shards, piece, 2 * HD),
        ],
        axis=1,
    )
    returned = exchange(packed_grads)
    returned_far = returned[:, : capacity * BLOCK].reshape(shards, capacity, BLOCK, 2 * HD)
    global_piece = jnp.sum(returned[:, capacity * BLOCK :].astype(jnp.float32), axis=0)
    global_piece = jnp.broadcast_to(global_piece[None].astype(jnp.bfloat16), (shards, piece, 2 * HD))
    global_total = exchange(global_piece).reshape(G, BLOCK, 2 * HD).astype(jnp.float32)
    local_grads = local_grads + jnp.einsum(
        "dmq,dmtc->qtc",
        send_table.astype(jnp.bfloat16),
        returned_far,
        preferred_element_type=jnp.float32,
    )
    local_grads = local_grads.at[:G].add(
        jnp.where(myself == 0, global_total, jnp.zeros_like(global_total))
    )
    key_grad = local_grads[:, :, :HD].reshape(per_dev * BLOCK, HD).astype(jnp.bfloat16)
    value_grad = local_grads[:, :, HD:].reshape(per_dev * BLOCK, HD).astype(jnp.bfloat16)
    return (query_grad, key_grad, value_grad)

MESH = pl.DeviceIdType.MESH
LINE = 4
SHARD = QB_DEV * BLOCK


def place():
    me = lax.axis_index("ctx")
    return me // 4, (me // 2) % 2, me % 2


def index_of(z, y, c):
    return z * 4 + y * 2 + c


def remote(src, dst, send_sem, recv_sem, **device):
    return pltpu.make_async_remote_copy(
        src_ref=src, dst_ref=dst, send_sem=send_sem, recv_sem=recv_sem, device_id=device, device_id_type=MESH
    )


def greet(z, y, c, head):
    barrier = pltpu.get_barrier_semaphore()

    def tell(**device):
        pl.semaphore_signal(barrier, inc=1, device_id=device, device_id_type=MESH)

    tell(ctx=index_of(z, 1 - y, c))
    tell(ctx=index_of(z, y, 1 - c))
    if head is not None:
        tell(head=1 - head)

    @pl.when(z > 0)
    def _():
        tell(ctx=index_of(z - 1, y, c))

    @pl.when(z < LINE - 1)
    def _():
        tell(ctx=index_of(z + 1, y, c))

    peers = (2 if head is None else 3) + (z + 2) // 3 + (5 - z) // 3
    pl.semaphore_wait(barrier, peers)


def gather_kernel(
    q_in, k_in, v_in, g_in, q_out, g_out, pool,
    local_sem, head_send, head_recv, up_send, down_send, y_send, c_send, z_recv, y_recv, c_recv,
):
    z, y, c = place()
    me = index_of(z, y, c)
    head = lax.axis_index("head")
    other = 1 - head
    tokens = k_in.shape[0]

    def half(zz, yy, u):
        start = index_of(zz, yy, c) * SHARD + u * tokens
        return pool.at[pl.ds(pl.multiple_of(start, tokens), tokens), :]

    pool_rows = pl.ds(pl.multiple_of(me * SHARD + head * tokens, tokens), tokens)
    out_rows = pl.ds(pl.multiple_of(head * tokens, tokens), tokens)
    jobs = []
    for src, dst, width in (
        (k_in, pool.at[pool_rows, :HD], HD),
        (v_in, pool.at[pool_rows, HD:], HD),
        (q_in, q_out.at[out_rows, :], GROUP * HD),
        (g_in, g_out.at[out_rows, :], GROUP * HD),
    ):
        i = len(jobs)
        mine = src.at[:, pl.ds(pl.multiple_of(head * width, width), width)]
        theirs = src.at[:, pl.ds(pl.multiple_of(other * width, width), width)]
        jobs.append(
            (
                pltpu.make_async_copy(mine, dst, local_sem.at[i]),
                remote(theirs, dst, head_send.at[i], head_recv.at[i], head=other),
            )
        )
    for local, _ in jobs:
        local.start()
    greet(z, y, c, head)
    for _, away in jobs[:2]:
        away.start()

    def up(zz, u):
        part = half(zz, y, u)
        slot = zz * 2 + u
        return remote(part, part, up_send.at[slot], z_recv.at[slot], ctx=index_of((z + 1) % LINE, y, c))

    def down(zz, u):
        part = half(zz, y, u)
        slot = zz * 2 + u
        return remote(part, part, down_send.at[slot], z_recv.at[slot], ctx=index_of((z + 3) % LINE, y, c))

    def across(zz, u):
        part = half(zz, y, u)
        slot = zz * 2 + u
        return remote(part, part, y_send.at[slot], y_recv.at[slot], ctx=index_of(z, 1 - y, c))

    def beside(zz, yy, u):
        part = half(zz, yy, u)
        slot = zz * 4 + yy * 2 + u
        return remote(part, part, c_send.at[slot], c_recv.at[slot], ctx=index_of(z, y, 1 - c))

    def pass_on(zz, u, upward, downward):
        if upward:

            @pl.when(z < LINE - 1)
            def _():
                up(zz, u).start()

        if downward:

            @pl.when(z > 0)
            def _():
                down(zz, u).start()

        across(zz, u).start()
        beside(zz, y, u).start()

    for local, _ in jobs[:2]:
        local.wait()
    pass_on(z, head, True, True)
    for _, away in jobs[:2]:
        away.wait_recv()
    pass_on(z, other, True, True)
    for _, away in jobs[2:]:
        away.start()

    def from_partner(zz, u):
        across(zz, u).wait_recv()
        beside(zz, 1 - y, u).start()

    def from_below(zz, u):
        up(zz, u).wait_recv()
        pass_on(zz, u, True, False)

    def from_above(zz, u):
        down(zz, u).wait_recv()
        pass_on(zz, u, False, True)

    def stage(j, u, below, above):
        @pl.when(z - j >= 0)
        def _():
            below(z - j, u)

        @pl.when(z + j <= LINE - 1)
        def _():
            above(z + j, u)

    for j in range(1, LINE):
        for u in (head, other):
            stage(j, u, from_below, from_above)
            if j == 1:
                from_partner(z, u)
            else:
                stage(j - 1, u, from_partner, from_partner)
    for u in (head, other):
        stage(LINE - 1, u, from_partner, from_partner)

    for zz in range(LINE):
        for u in range(2):
            for yy in range(2):
                beside(zz, yy, u).wait_recv()
                beside(zz, yy, u).wait_send()
            across(zz, u).wait_send()

            @pl.when((z < LINE - 1) & (zz <= z))
            def _():
                up(zz, u).wait_send()

            @pl.when((z > 0) & (zz >= z))
            def _():
                down(zz, u).wait_send()

    for i, (local, away) in enumerate(jobs):
        if i >= 2:
            local.wait()
            away.wait_recv()
        away.wait_send()


def gather(queries, keys, values, grads, total_blocks):
    anywhere = pl.BlockSpec(memory_space=pl.ANY)
    tokens = queries.shape[0]
    moved = jax.ShapeDtypeStruct((2 * tokens, GROUP * HD), jnp.bfloat16)
    dma = pltpu.SemaphoreType.DMA
    return pl.pallas_call(
        gather_kernel,
        in_specs=[anywhere] * 4,
        out_specs=[anywhere] * 3,
        out_shape=[moved, moved, jax.ShapeDtypeStruct((total_blocks * BLOCK, 2 * HD), jnp.bfloat16)],
        scratch_shapes=[
            dma((4,)), dma((4,)), dma((4,)), dma((2 * LINE,)), dma((2 * LINE,)), dma((2 * LINE,)), dma((4 * LINE,)),
            dma((2 * LINE,)), dma((2 * LINE,)), dma((4 * LINE,)),
        ],
        compiler_params=pltpu.CompilerParams(collective_id=0, has_side_effects=True),
        name="gather",
    )(queries, keys, values, grads)


def reduce_kernel(
    grads, local_hbm, key_grad, value_grad,
    held, local, c_in, y_out, y_in, z_out, z_in, h_sem, c_send, c_recv, y_send, y_recv, z_send, z_recv,
):
    z, y, c = place()
    size = SHARD // 2

    def rows_of(zz, yy, cc, u):
        return pl.multiple_of(index_of(zz, yy, cc) * SHARD + u * size, size)

    def beside(zz, yy, u):
        slot = zz * 4 + yy * 2 + u
        part = grads.at[pl.ds(rows_of(zz, yy, 1 - c, u), size), :]
        return remote(part, c_in.at[slot], c_send.at[slot], c_recv.at[slot], ctx=index_of(z, y, 1 - c))

    def across(zz, u):
        slot = zz * 2 + u
        return remote(
            y_out.at[slot], y_in.at[slot], y_send.at[slot], y_recv.at[slot], ctx=index_of(z, 1 - y, c)
        )

    def up(zz, u):
        slot = zz * 2 + u
        return remote(
            z_out.at[slot], z_in.at[0, slot], z_send.at[slot], z_recv.at[0, slot],
            ctx=index_of((z + 1) % LINE, y, c),
        )

    def down(zz, u):
        slot = zz * 2 + u
        return remote(
            z_out.at[slot], z_in.at[1, slot], z_send.at[slot], z_recv.at[1, slot],
            ctx=index_of((z + 3) % LINE, y, c),
        )

    def pick(options):
        return jnp.where(z == 0, options[0], jnp.where(z == 1, options[1], jnp.where(z == 2, options[2], options[3])))

    order = [pick(options) for options in ((3, 3, 0, 0), (2, 0, 3, 1), (1, 2, 1, 2))] + [z]
    units = [(zz, u) for zz in order for u in range(2)]

    def send_beside(i):
        if i < len(units):
            beside(units[i][0], 1 - y, units[i][1]).start()
            beside(units[i][0], y, units[i][1]).start()

    def hold(zz, yy):
        part = grads.at[pl.ds(rows_of(zz, yy, c, 0), SHARD), :]
        return pltpu.make_async_copy(part, held.at[zz * 2 + yy], h_sem.at[zz * 2 + yy])

    hold_local = pltpu.make_async_copy(local_hbm, local, h_sem.at[2 * LINE])

    def tiles(body):
        @pl.loop(0, size // BLOCK)
        def _(i):
            body(pl.multiple_of(i * BLOCK, BLOCK))

    def fold_across(i):
        zz, u = units[i]
        if u == 0:
            hold(zz, 1 - y).wait()
        beside(zz, 1 - y, u).wait_recv()

        def fold(row):
            mine = held[zz * 2 + 1 - y, pl.ds(u * size + row, BLOCK), :].astype(jnp.float32)
            theirs = c_in[zz * 4 + (1 - y) * 2 + u, pl.ds(row, BLOCK), :].astype(jnp.float32)
            y_out[zz * 2 + u, pl.ds(row, BLOCK), :] = (mine + theirs).astype(jnp.bfloat16)

        tiles(fold)
        if i >= 2:
            across(*units[i - 2]).wait_send()
        across(zz, u).start()

    def along(i):
        zz, u = units[i]
        slot = zz * 2 + u
        if u == 0:
            hold(zz, y).wait()
        beside(zz, y, u).wait_recv()
        across(zz, u).wait_recv()

        def gathered(row, mine):
            theirs = c_in[zz * 4 + y * 2 + u, pl.ds(row, BLOCK), :].astype(jnp.float32)
            return mine + theirs + y_in[slot, pl.ds(row, BLOCK), :].astype(jnp.float32)

        def part(side, row):
            return z_in[side, slot, pl.ds(row, BLOCK), :].astype(jnp.float32)

        if i >= len(units) - 2:
            own = u * size
            if u == 0:
                hold_local.wait()

            def finish(*sides):
                def body(row):
                    rows = pl.ds(pl.multiple_of(own + row, BLOCK), BLOCK)
                    total = gathered(row, local[rows, :])
                    for side in sides:
                        total += part(side, row)
                    key_grad[rows, :] = total[:, :HD].astype(jnp.bfloat16)
                    value_grad[rows, :] = total[:, HD:].astype(jnp.bfloat16)

                tiles(body)

            @pl.when(z == 0)
            def _():
                down(zz, u).wait_recv()
                finish(1)

            @pl.when(z == LINE - 1)
            def _():
                up(zz, u).wait_recv()
                finish(0)

            @pl.when((z > 0) & (z < LINE - 1))
            def _():
                up(zz, u).wait_recv()
                down(zz, u).wait_recv()
                finish(0, 1)

            return

        def extend(*sides):
            def body(row):
                total = gathered(row, held[zz * 2 + y, pl.ds(u * size + row, BLOCK), :].astype(jnp.float32))
                for side in sides:
                    total += part(side, row)
                z_out[slot, pl.ds(row, BLOCK), :] = total.astype(jnp.bfloat16)

            tiles(body)

        @pl.when((z == 0) | (z == LINE - 1))
        def _():
            extend()

        @pl.when((z > 0) & (z < LINE - 1) & (zz > z))
        def _():
            up(zz, u).wait_recv()
            extend(0)

        @pl.when((z > 0) & (z < LINE - 1) & (zz < z))
        def _():
            down(zz, u).wait_recv()
            extend(1)

        @pl.when(zz > z)
        def _():
            up(zz, u).start()

        @pl.when(zz < z)
        def _():
            down(zz, u).start()

    for zz in order:
        hold(zz, 1 - y).start()
        hold(zz, y).start()
    hold_local.start()
    greet(z, y, c, None)
    send_beside(0)
    send_beside(1)
    for i in range(len(units) + 2):
        if i < len(units):
            fold_across(i)
            send_beside(i + 2)
        if i >= 2:
            along(i - 2)

    for i, (zz, u) in enumerate(units):
        beside(zz, 0, u).wait_send()
        beside(zz, 1, u).wait_send()
        if i >= len(units) - 2:
            across(zz, u).wait_send()
        else:
            up(zz, u).wait_send()


def reduce(grads, local):
    in_vmem = pl.BlockSpec(memory_space=pltpu.VMEM)
    dma = pltpu.SemaphoreType.DMA
    part = (SHARD // 2, 2 * HD)
    result = jax.ShapeDtypeStruct((SHARD, HD), jnp.bfloat16)
    return pl.pallas_call(
        reduce_kernel,
        in_specs=[pl.BlockSpec(memory_space=pl.ANY)] * 2,
        out_specs=[in_vmem] * 2,
        out_shape=[result, result],
        scratch_shapes=[
            pltpu.VMEM((2 * LINE, SHARD, 2 * HD), jnp.bfloat16),
            pltpu.VMEM((SHARD, 2 * HD), jnp.float32),
            pltpu.VMEM((4 * LINE, *part), jnp.bfloat16),
            pltpu.VMEM((2 * LINE, *part), jnp.bfloat16),
            pltpu.VMEM((2 * LINE, *part), jnp.bfloat16),
            pltpu.VMEM((2 * LINE, *part), jnp.bfloat16),
            pltpu.VMEM((2, 2 * LINE, *part), jnp.bfloat16),
            dma((2 * LINE + 1,)), dma((4 * LINE,)), dma((4 * LINE,)), dma((2 * LINE,)), dma((2 * LINE,)), dma((2 * LINE,)), dma((2, 2 * LINE)),
        ],
        compiler_params=pltpu.CompilerParams(
            collective_id=1, has_side_effects=True, vmem_limit_bytes=62 << 20
        ),
        name="reduce",
    )(grads, local)


def body_line(queries, keys, values, out_grad, rand_blocks, rand_count):
    total_blocks = rand_blocks.shape[0]
    head_queries, head_grads, pool = gather(queries, keys, values, out_grad, total_blocks)
    pool = pool.reshape(total_blocks, BLOCK, 2 * HD)
    query_grad, local_grads, all_grads = attend(
        rand_blocks.T, rand_count, head_queries, head_grads, pool, direct=True
    )
    key_grad, value_grad = reduce(
        all_grads.reshape(total_blocks * BLOCK, 2 * HD), local_grads.reshape(SHARD, 2 * HD)
    )
    return (query_grad, key_grad, value_grad)


def solution(mesh):
    line = mesh.shape["ctx"] == 4 * LINE and mesh.shape["head"] == 2
    placed = P(("ctx", "head"), None)
    return jax.shard_map(
        body_line if line else body,
        mesh=mesh,
        in_specs=(placed, placed, placed, placed, P(), P()),
        out_specs=(P("ctx", "head"), P("ctx", "head"), P("ctx", "head")),
        check_vma=False,
    )
```
